32 devices in a mesh: ty: 4 (over x, core), tx: 8 (over z, y).
Axes of the slice: x: 2, y: 2, z: 4, core: 2. Of those that a mesh axis runs over, the one named last changes fastest.
Arguments:
- tiles: bfloat16 [4, 8, 4, 512, 512], P('ty', 'tx'), may hold values from -6 to 6
- shifts: int32 [4, 8, 2], P('ty', 'tx'), may hold values from -28 to 28
- piece_target: int32 [4, 8, 256], P('ty', 'tx'), may hold values from 0 to 2047, as said below
- coarse_target: int32 [4, 8, 64], P('ty', 'tx'), may hold values from 0 to 511, as said below
Outputs:
- joined: bfloat16 [2048, 4096], P(('ty', 'tx'))
- coarse: bfloat16 [512, 256], P(('ty', 'tx'))
- corr_right: float32 [48, 1024], P('ty', 'tx')
- corr_below: float32 [48, 1024], P('ty', 'tx')
The draws below stay inside these ranges and needn't reach their ends.
Inputs may be any that keep to these rules, and one draw needn't show every extreme that they name: `piece_target`: each tile sends at most 16 sub-blocks to the sub-blocks of one owner device; in every draw some owner devices receive exactly 16 from every tile. `coarse_target`: owners lie in the same tile row; every device sends exactly 8 pieces to each device of its row, and every target of every device is named exactly once.
All inputs are finite; a program needn't handle non-finite values.
Results may differ from the reference program's by a relative error of at most 0.008.
Values may be sent and summed in bfloat16 or wider, within the bound.
A program may use at most 128 MiB of HBM per device.

```python
import math
import jax
import jax.numpy as jnp
from jax import lax

TS = 512
TILE_SLICES = 4
SUBBLOCK_SIDE = 32
OV = 48
H = 8
DEVICE_SUBBLOCKS = 64
NP = 256
CAP = 16
N_TY = 4
N_TX = 8


def draw_piece_target(key, part):
    count_all = N_TY * N_TX
    order = jax.random.permutation(jax.random.fold_in(key, 11), count_all)
    hottest = order[:count_all // 8]
    others = order[count_all // 8:]

    def per_device(device):
        dev_key = jax.random.fold_in(jax.random.fold_in(key, 12), device)
        mixed = jax.random.permutation(jax.random.fold_in(dev_key, 1), others)
        owners = jnp.concatenate([jnp.repeat(hottest, CAP), jnp.repeat(mixed[:count_all // 4], CAP // 4), jnp.repeat(mixed[count_all // 4:], CAP // 2)])
        owners = jax.random.permutation(jax.random.fold_in(dev_key, 2), owners)
        slot_ids = jax.random.randint(jax.random.fold_in(dev_key, 3), (NP,), 0, DEVICE_SUBBLOCKS)
        return owners * DEVICE_SUBBLOCKS + slot_ids
    drawn = jax.vmap(per_device)(jnp.arange(count_all))
    return drawn.reshape(N_TY, N_TX, NP).astype(jnp.int32)


def draw_coarse_target(key, part):
    per_peer = DEVICE_SUBBLOCKS // N_TX

    def per_row(row):
        row_key = jax.random.fold_in(jax.random.fold_in(key, 21), row)
        offsets = jax.random.permutation(jax.random.fold_in(row_key, 0), N_TX)
        orders = jax.vmap(lambda owner: jax.random.permutation(jax.random.fold_in(row_key, owner + 1), DEVICE_SUBBLOCKS))(jnp.arange(N_TX))
        fine_slot = jnp.arange(DEVICE_SUBBLOCKS)[None, :]
        source = jnp.arange(N_TX)[:, None]
        owner_col = (fine_slot + offsets[:, None]) % N_TX
        within = source * per_peer + fine_slot // N_TX
        chosen = orders[owner_col, within]
        return owner_col * DEVICE_SUBBLOCKS + chosen
    drawn = jax.vmap(per_row)(jnp.arange(N_TY))
    return drawn.reshape(N_TY, N_TX, DEVICE_SUBBLOCKS).astype(jnp.int32)


def plant(result, own_key, least, high):
    longest = result.shape.index(max(result.shape))
    spots = []
    for shift in (0, 1):
        where = [jax.random.randint(jax.random.fold_in(own_key, axis), (), 0, length) for axis, length in enumerate(result.shape)]
        where[longest] = (where[longest] + shift) % result.shape[longest]
        spots.append(tuple(where))
    return result.at[spots[0]].set(least).at[spots[1]].set(high)


def block_scale(rng, shape, shards, smallest, high):
    factor_of = 1.0
    for position, blocks in shards:
        heights = jax.random.uniform(jax.random.fold_in(jax.random.fold_in(rng, 6), position), (blocks,), jnp.float32, smallest / len(shards), high / len(shards))
        factor_of = factor_of * jnp.repeat(jnp.exp(heights), shape[position] // blocks).reshape((-1,) + (1,) * (len(shape) - 1 - position))
    return factor_of


def noise(key, shape, scale, bound, split=(), held_as=jnp.bfloat16):
    level = block_scale(key, shape, split, -0.22, 0.18) if split else 1.0
    entries = jax.random.normal(key, shape, jnp.float32) * scale * level
    return jnp.minimum(jnp.maximum(entries, -bound), bound).astype(held_as)


def setup_inputs(seed: int = 0) -> dict:
    splits = jax.random.split(jax.random.key(seed), 5)
    tiles = noise(splits[0], (N_TY, N_TX, TILE_SLICES, TS, TS), 1.0, 6.0, ((0, 4), (1, 8)))
    shifts = plant(jax.random.randint(splits[1], (N_TY, N_TX, 2), 4 - 4 * H, 4 * H - 3), jax.random.fold_in(splits[1], 1), 4 - 4 * H, (4 * H - 3) - 1).astype(jnp.int32)
    piece_target = draw_piece_target(jax.random.fold_in(splits[4], 71), 0)
    coarse_target = draw_coarse_target(jax.random.fold_in(splits[4], 71), 0)
    return dict(tiles=tiles, shifts=shifts, piece_target=piece_target, coarse_target=coarse_target)


def bin_columns(strips):
    lead = strips.shape[:-3]
    voxel_values = strips.astype(jnp.float32).reshape(lead + (TILE_SLICES, TS // 4, 4, OV // 4, 4))
    summed = lax.optimization_barrier(jnp.sum(voxel_values, axis=(-5, -3, -1)))
    return jnp.swapaxes(summed, -1, -2) * (1.0 / math.sqrt(16.0 * TILE_SLICES))

def bin_rows(strips):
    lead = strips.shape[:-3]
    voxel_values = strips.astype(jnp.float32).reshape(lead + (TILE_SLICES, OV // 4, 4, TS // 4, 4))
    return lax.optimization_barrier(jnp.sum(voxel_values, axis=(-5, -3, -1))) * (1.0 / math.sqrt(16.0 * TILE_SLICES))

def phase_surface(own, other):
    own_spec = jnp.fft.fft2(own, norm='ortho')
    other_spec = jnp.fft.fft2(other, norm='ortho')
    cross = own_spec * jnp.conj(other_spec)
    normed = cross / jnp.sqrt(jnp.real(cross) ** 2 + jnp.imag(cross) ** 2 + 1.0)
    return jnp.real(jnp.fft.ifft2(normed, norm='ortho')).astype(jnp.float32)

def layout(surfaces):
    return surfaces.transpose(0, 2, 1, 3).reshape(N_TY * (OV // 4), N_TX * (TS // 4))

def ramp_weights():
    index = jnp.arange(TS, dtype=jnp.int32)
    nearest = jnp.minimum(jnp.minimum(index + 1, TS - index), OV).astype(jnp.float32)
    ramp = 1.0 + 3.0 * nearest / OV
    return ramp[:, None] * ramp[None, :]

def shift_axis(voxel_values, shift, axis):
    whole = jnp.floor_divide(shift, 4)
    frac = (shift - 4 * whole).astype(jnp.float32) * 0.25
    start = (whole + H).astype(jnp.int32)
    first = lax.dynamic_slice_in_dim(voxel_values, start, TS, axis).astype(jnp.float32)
    second = lax.dynamic_slice_in_dim(voxel_values, start + 1, TS, axis).astype(jnp.float32)
    return (1.0 - frac) * first + frac * second

def to_pieces(volume):
    slice_depth = volume.shape[0]
    grid_side = TS // SUBBLOCK_SIDE
    shaped = volume.reshape(slice_depth, grid_side, SUBBLOCK_SIDE, grid_side, SUBBLOCK_SIDE).transpose(1, 3, 0, 2, 4)
    return shaped.reshape(grid_side * grid_side, slice_depth * SUBBLOCK_SIDE * SUBBLOCK_SIDE)

def reduce_resolution(voxel_values):
    count, slice_depth, height, width = voxel_values.shape
    shaped = voxel_values.astype(jnp.float32).reshape(count, slice_depth // 2, 2, height // 2, 2, width // 2, 2)
    return lax.optimization_barrier(jnp.sum(shaped, axis=(2, 4, 6))) * 0.125

def assemble(quadrant_blocks):
    count, slice_depth, height, width = quadrant_blocks.shape
    shaped = quadrant_blocks.reshape(count // 4, 2, 2, slice_depth, height, width).transpose(0, 3, 1, 4, 2, 5)
    return shaped.reshape(count // 4, slice_depth * 4 * height * width)

def reference(tiles, shifts, piece_target, coarse_target):
    right_bins = bin_columns(tiles[..., TS - OV:])
    left_bins = bin_columns(tiles[..., :OV])
    bottom_bins = bin_rows(tiles[..., TS - OV:, :])
    top_bins = bin_rows(tiles[..., :OV, :])
    next_left = jnp.concatenate([left_bins[:, 1:], jnp.zeros_like(left_bins[:, :1])], axis=1)
    next_top = jnp.concatenate([top_bins[1:], jnp.zeros_like(top_bins[:1])], axis=0)
    corr_right = layout(phase_surface(right_bins, next_left))
    corr_below = layout(phase_surface(bottom_bins, next_top))
    device_list = N_TY * N_TX
    placed_grid = tiles.transpose(2, 0, 3, 1, 4).reshape(TILE_SLICES, N_TY * TS, N_TX * TS)
    padded = jnp.pad(placed_grid, ((0, 0), (H, H), (H, H)))
    weights = ramp_weights()
    weight_pieces = to_pieces(weights.astype(jnp.bfloat16)[None]).astype(jnp.float32)
    targets = piece_target.reshape(device_list, -1)

    def accumulate(carry, index):
        numer, denom = carry
        row = (index // N_TX).astype(jnp.int32)
        column = (index % N_TX).astype(jnp.int32)
        extended = lax.dynamic_slice(padded, (jnp.int32(0), row * TS, column * TS), (TILE_SLICES, TS + 2 * H, TS + 2 * H))
        along_y = shift_axis(extended, shifts[row, column, 0], 1).astype(jnp.bfloat16)
        resampled = shift_axis(along_y, shifts[row, column, 1], 2)
        weighted = (weights[None] * resampled).astype(jnp.bfloat16)
        pieces = to_pieces(weighted).astype(jnp.float32)
        chosen = targets[index]
        numer = numer.at[chosen].add(pieces)
        denom = denom.at[chosen].add(weight_pieces)
        return ((numer, denom), None)
    numer0 = jnp.zeros((device_list * DEVICE_SUBBLOCKS, TILE_SLICES * SUBBLOCK_SIDE * SUBBLOCK_SIDE), jnp.float32)
    denom0 = jnp.zeros((device_list * DEVICE_SUBBLOCKS, SUBBLOCK_SIDE * SUBBLOCK_SIDE), jnp.float32)
    (numer, denom), _ = lax.scan(accumulate, (numer0, denom0), jnp.arange(device_list, dtype=jnp.int32))
    joined = (numer.reshape(device_list * DEVICE_SUBBLOCKS, TILE_SLICES, SUBBLOCK_SIDE * SUBBLOCK_SIDE) / jnp.maximum(denom, 1.0)[:, None, :]).astype(jnp.bfloat16)
    first_level = reduce_resolution(joined.reshape(device_list * DEVICE_SUBBLOCKS, TILE_SLICES, SUBBLOCK_SIDE, SUBBLOCK_SIDE)).astype(jnp.bfloat16)
    quadrant_blocks = reduce_resolution(first_level)
    flat_target = coarse_target.reshape(-1)
    source_dev = jnp.arange(device_list * DEVICE_SUBBLOCKS, dtype=jnp.int32) // DEVICE_SUBBLOCKS
    destination = (source_dev // N_TX * N_TX + flat_target // DEVICE_SUBBLOCKS) * DEVICE_SUBBLOCKS + flat_target % DEVICE_SUBBLOCKS
    positioned_tiles = jnp.zeros_like(quadrant_blocks).at[destination].set(quadrant_blocks)
    coarse = assemble(positioned_tiles).astype(jnp.bfloat16)
    return (joined.reshape(device_list * DEVICE_SUBBLOCKS, TILE_SLICES * SUBBLOCK_SIDE * SUBBLOCK_SIDE), coarse, corr_right, corr_below)
```

```python
import functools
import math

import jax
import jax.numpy as jnp
from jax import lax
from jax.experimental import pallas as pl
from jax.experimental.pallas import tpu as pltpu
from jax.sharding import PartitionSpec as P

SIDE = 32
OV = 48
H = 8
SLOTS = 64
LANES = 128
GROUPS = LANES // SIDE
F32 = jnp.float32
BF16 = jnp.bfloat16


def shifted(value, axis, steps):
    count = lax.axis_size(axis)
    first, last = (max(0, -steps), min(count, count - steps))
    return lax.ppermute(value, axis, [(source, source + steps) for source in range(first, last)])


def highest(left, right):
    return jnp.dot(left, right, precision=lax.Precision.HIGHEST, preferred_element_type=F32)


def iota(shape, dim):
    return lax.broadcasted_iota(jnp.int32, shape, dim)


def mm(a, b):
    return jnp.dot(a, b, preferred_element_type=F32)


def mm_t(a, b):
    return lax.dot_general(a, b, (((1,), (1,)), ((), ())), preferred_element_type=F32)


def bins_kernel(tile_ref, right_ref, left_ref, bottom_ref, top_ref):
    depth, length, _ = tile_ref.shape
    bins = OV // 4
    scale = 1.0 / math.sqrt(16.0 * depth)
    pool = (iota((length, length // 4), 0) // 4 == iota((length, length // 4), 1)).astype(F32)
    first = (iota((16, LANES), 1) // 4 == iota((16, LANES), 0)).astype(BF16)
    last = ((iota((16, LANES), 1) - (LANES - OV)) // 4 == iota((16, LANES), 0)) & (
        iota((16, LANES), 1) >= LANES - OV
    )
    last = last.astype(BF16)
    left = right = top = bottom = jnp.zeros((16, length), F32)
    for z in range(depth):
        left += mm_t(first, tile_ref[z, :, :LANES])
        right += mm_t(last, tile_ref[z, :, length - LANES :])
        top += mm(first, tile_ref[z, :LANES, :])
        bottom += mm(last, tile_ref[z, length - LANES :, :])
    for ref, value in ((right_ref, right), (left_ref, left), (bottom_ref, bottom), (top_ref, top)):
        ref[...] = highest(value, pool)[:bins] * scale


def all_bins(tile):
    length = tile.shape[1]
    shape = jax.ShapeDtypeStruct((OV // 4, length // 4), F32)
    vmem = pl.BlockSpec(memory_space=pltpu.VMEM)
    return pl.pallas_call(
        bins_kernel,
        out_shape=[shape] * 4,
        in_specs=[vmem],
        out_specs=[vmem] * 4,
        name="bins",
        cost_estimate=pl.CostEstimate(flops=10**8, bytes_accessed=2**21, transcendentals=0),
    )(tile)


def dft_tables(length):
    index = jnp.arange(length, dtype=jnp.int32)
    product = index[:, None] * index[None, :] % length
    angle = product.astype(F32) * (2.0 * math.pi / length)
    norm = 1.0 / math.sqrt(length)
    return (jnp.cos(angle) * norm, jnp.sin(angle) * norm)


def phase_kernel(ca_ref, sa_ref, cb_ref, sb_ref, r_ref, l_ref, b_ref, t_ref, right_ref, below_ref):
    cos_a, sin_a, cos_b, sin_b = ca_ref[...], sa_ref[...], cb_ref[...], sb_ref[...]

    def spectrum(values):
        left_cos = highest(cos_a, values)
        left_sin = highest(sin_a, values)
        re = highest(left_cos, cos_b) - highest(left_sin, sin_b)
        im = -(highest(left_cos, sin_b) + highest(left_sin, cos_b))
        return (re, im)

    for own_ref, other_ref, out_ref in ((r_ref, l_ref, right_ref), (b_ref, t_ref, below_ref)):
        own_re, own_im = spectrum(own_ref[...])
        other_re, other_im = spectrum(other_ref[...])
        cross_re = own_re * other_re + own_im * other_im
        cross_im = own_im * other_re - own_re * other_im
        scale = 1.0 / jnp.sqrt(cross_re * cross_re + cross_im * cross_im + 1.0)
        normed_re = cross_re * scale
        normed_im = cross_im * scale
        out = highest(highest(cos_a, normed_re) - highest(sin_a, normed_im), cos_b)
        out = out - highest(highest(sin_a, normed_re) + highest(cos_a, normed_im), sin_b)
        out_ref[...] = out


def phase_surfaces(right, left, bottom, top):
    rows, columns = right.shape
    pad = 16 - rows
    cos_a, sin_a = (jnp.pad(t, ((0, pad), (0, pad))) for t in dft_tables(rows))
    cos_b, sin_b = dft_tables(columns)
    padded = [jnp.pad(v, ((0, pad), (0, 0))) for v in (right, left, bottom, top)]
    vmem = pl.BlockSpec(memory_space=pltpu.VMEM)
    out = pl.pallas_call(
        phase_kernel,
        out_shape=[jax.ShapeDtypeStruct((16, columns), F32)] * 2,
        in_specs=[vmem] * 8,
        out_specs=[vmem] * 2,
        name="phase",
        cost_estimate=pl.CostEstimate(flops=10**8, bytes_accessed=2**18, transcendentals=4096),
    )(cos_a, sin_a, cos_b, sin_b, *padded)
    return out[0][:rows], out[1][:rows]


def swap_groups(parts):
    group = iota(parts[0].shape, 1) // SIDE

    def pick(choices):
        value = choices[3]
        for g in range(3):
            value = jnp.where(group == g, choices[g], value)
        return value

    turned = []
    for d in range(GROUPS):
        mixed = pick([parts[(g + d) % GROUPS] for g in range(GROUPS)])
        turned.append(pltpu.roll(mixed, d * SIDE, 1) if d else mixed)
    return [pick([turned[(j - g) % GROUPS] for j in range(GROUPS)]) for g in range(GROUPS)]


def taps(offset, shape, out_dim, column):
    whole, frac = offset
    at = iota(shape, out_dim) + whole + H
    return (
        jnp.where(column == at, 1.0 - frac, 0.0) + jnp.where(column == at + 1, frac, 0.0)
    ).astype(BF16)


def split_shift(shift):
    whole = lax.shift_right_arithmetic(shift, 2)
    return whole, (shift - 4 * whole).astype(F32) * 0.25


def ramp(shape, dim, length):
    index = iota(shape, dim)
    nearest = jnp.minimum(jnp.minimum(index + 1, length - index), OV).astype(F32)
    return 1.0 + 3.0 * nearest / OV


def pieces_kernel(shift_ref, pos_ref, tile_ref, tb_ref, side_ref, corner_ref, send_ref, work_ref):
    depth, length, _ = tile_ref.shape

    def edge_column(shape, dim):
        c = iota(shape, dim)
        return jnp.where(c < H, c, c + length)

    sy, sx = split_shift(shift_ref[0]), split_shift(shift_ref[1])
    full, thin, wide = (length, length), (length, 2 * H), (2 * H, length)
    ry = taps(sy, full, 0, iota(full, 1) + H)
    ry_edge = taps(sy, thin, 0, edge_column(thin, 1))
    rx = taps(sx, full, 1, iota(full, 0) + H)
    rx_edge = taps(sx, wide, 1, edge_column(wide, 0))
    weights = ramp((length, 1), 0, length) * ramp((1, length), 1, length)
    for z in range(depth):
        along = (mm(ry, tile_ref[z]) + mm(ry_edge, tb_ref[z])).astype(BF16)
        along_side = (mm_t(ry, side_ref[z]) + mm_t(ry_edge, corner_ref[z])).astype(BF16)
        resampled = mm(along, rx) + mm(along_side, rx_edge)
        work_ref[z] = weights * resampled
    send_ref[...] = jnp.zeros_like(send_ref)
    grid_side = length // SIDE

    def row(py, carry):
        start = pl.multiple_of(py * SIDE, SIDE)
        for q in range(length // LANES):
            parts = [work_ref[z, pl.ds(start, SIDE), q * LANES : (q + 1) * LANES] for z in range(depth)]
            for g, piece in enumerate(swap_groups(parts)):
                send_ref[pos_ref[py * grid_side + q * GROUPS + g]] = piece.astype(BF16)
        return carry

    lax.fori_loop(0, grid_side, row, 0)


def make_pieces(shifts, position, tile, tb, side, corner, rows):
    vmem = pl.BlockSpec(memory_space=pltpu.VMEM)
    smem = pl.BlockSpec(memory_space=pltpu.SMEM)
    return pl.pallas_call(
        pieces_kernel,
        out_shape=jax.ShapeDtypeStruct((rows, SIDE, LANES), BF16),
        in_specs=[smem, smem, vmem, vmem, vmem, vmem],
        out_specs=vmem,
        scratch_shapes=[pltpu.VMEM(tile.shape, F32)],
        name="pieces",
        compiler_params=pltpu.CompilerParams(vmem_limit_bytes=40 * 2**20),
        cost_estimate=pl.CostEstimate(flops=2 * 10**9, bytes_accessed=2**23, transcendentals=0),
    )(shifts, position, tile, tb, side, corner)


def join_kernel(slot_ref, got_ref, denom_ref, joined_ref, quads_ref, acc_ref, mean_ref):
    acc_ref[...] = jnp.zeros_like(acc_ref)

    def add(i, carry):
        slot = slot_ref[i]

        @pl.when(slot < SLOTS)
        def _():
            acc_ref[slot] = acc_ref[slot] + got_ref[i].astype(F32)

        return carry

    lax.fori_loop(0, got_ref.shape[0], add, 0, unroll=4)
    row = iota((LANES, LANES), 0)
    column = iota((LANES, LANES), 1)
    half = SIDE // 2
    pool_one = ((row // (2 * SIDE)) * half + (row % SIDE) // 2 == column).astype(BF16)
    pool_two = (((row % half) // 2 == column) & (row < SIDE)).astype(BF16)

    def finish(s, carry):
        value = (acc_ref[s] / jnp.maximum(denom_ref[s], 1.0)).astype(BF16)
        acc_ref[s] = value.astype(F32)
        mean_ref[...] = mm(value, pool_one)
        level = (mean_ref[pl.ds(0, half, stride=2), :] + mean_ref[pl.ds(1, half, stride=2), :]) * 0.125
        mean_ref[pl.ds(0, half), :] = mm(level.astype(BF16), pool_two)
        quads_ref[s] = (
            mean_ref[pl.ds(0, half // 2, stride=2), :] + mean_ref[pl.ds(1, half // 2, stride=2), :]
        ) * 0.125
        return carry

    lax.fori_loop(0, SLOTS, finish, 0, unroll=2)

    def restore(s, carry):
        rows = SIDE // GROUPS
        parts = [acc_ref[s, pl.ds(j, rows, stride=GROUPS), :] for j in range(GROUPS)]
        joined_ref[s] = jnp.concatenate(swap_groups(parts), axis=0).astype(BF16)
        return carry

    lax.fori_loop(0, SLOTS, restore, 0, unroll=2)


def join(slots, got, denom):
    vmem = pl.BlockSpec(memory_space=pltpu.VMEM)
    smem = pl.BlockSpec(memory_space=pltpu.SMEM)
    return pl.pallas_call(
        join_kernel,
        out_shape=[
            jax.ShapeDtypeStruct((SLOTS, SIDE, LANES), BF16),
            jax.ShapeDtypeStruct((SLOTS, SIDE // 4, LANES), F32),
        ],
        in_specs=[smem, vmem, vmem],
        out_specs=[vmem, vmem],
        scratch_shapes=[pltpu.VMEM((SLOTS, SIDE, LANES), F32), pltpu.VMEM((SIDE, LANES), F32)],
        name="join",
        compiler_params=pltpu.CompilerParams(vmem_limit_bytes=32 * 2**20),
        cost_estimate=pl.CostEstimate(flops=10**8, bytes_accessed=2**23, transcendentals=0),
    )(slots, got, denom)


def assemble(quadrant_blocks):
    count, height, width = quadrant_blocks.shape
    shaped = quadrant_blocks.reshape(count // 4, 2, 2, height, width).transpose(0, 1, 3, 2, 4)
    return shaped.reshape(count // 4, 4 * height * width)


def patch_weights(length, depth):
    grid_side = length // SIDE
    index = jnp.arange(length, dtype=jnp.int32)
    nearest = jnp.minimum(jnp.minimum(index + 1, length - index), OV).astype(F32)
    line = (1.0 + 3.0 * nearest / OV).reshape(grid_side, SIDE)
    across = jnp.tile(line, (1, depth))
    blend = line[:, None, :, None] * across[None, :, None, :]
    return blend.astype(BF16).reshape(grid_side * grid_side, SIDE * depth * SIDE)


def per_device(tiles, shifts, piece_target, coarse_target):
    tile = tiles[0, 0]
    count_y = lax.axis_size("ty")
    count_x = lax.axis_size("tx")
    devices = count_y * count_x
    depth, length, _ = tile.shape
    pieces_n = (length // SIDE) ** 2
    capacity = 2 * pieces_n // devices
    me = lax.axis_index("ty") * count_x + lax.axis_index("tx")

    top = shifted(tile[:, length - H :, :], "ty", 1)
    bottom = shifted(tile[:, :H, :], "ty", -1)
    targets = piece_target[0, 0]
    owners = targets // SLOTS
    order = jnp.arange(pieces_n, dtype=jnp.int32)
    earlier = (owners[:, None] == owners[None, :]) & (order[None, :] < order[:, None])
    position = owners * capacity + jnp.sum(earlier.astype(jnp.int32), axis=1)
    gathered = lax.all_gather(targets, ("ty", "tx"))

    tb = jnp.concatenate([top, bottom], axis=1)
    last = jnp.concatenate([tile[:, :, length - H :], tb[:, :, length - H :]], axis=1)
    first = jnp.concatenate([tile[:, :, :H], tb[:, :, :H]], axis=1)
    left = shifted(last.transpose(0, 2, 1), "tx", 1)
    right = shifted(first.transpose(0, 2, 1), "tx", -1)
    side = jnp.concatenate([left, right], axis=1)
    send = make_pieces(
        shifts[0, 0], position, tile, tb, side[:, :, :length], side[:, :, length:], devices * capacity
    )
    got = lax.all_to_all(send, ("ty", "tx"), split_axis=0, concat_axis=0, tiled=True)

    right_bins, left_bins, bottom_bins, top_bins = all_bins(tile)
    next_left = shifted(left_bins, "tx", -1)
    next_top = shifted(top_bins, "ty", -1)
    corr_right, corr_below = phase_surfaces(right_bins, next_left, bottom_bins, next_top)

    mine = gathered // SLOTS == me
    local = gathered % SLOTS
    marks = mine.astype(jnp.int32)
    rank = jnp.cumsum(marks, axis=1) - marks
    chosen = mine[:, None, :] & (rank[:, None, :] == jnp.arange(capacity, dtype=jnp.int32)[None, :, None])
    slots = SLOTS + jnp.sum(jnp.where(chosen, local[:, None, :] - SLOTS, 0), axis=2)
    wanted = me * SLOTS + jnp.arange(SLOTS, dtype=jnp.int32)
    counts = jnp.sum((gathered[None] == wanted[:, None, None]).astype(F32), axis=1).astype(BF16)
    denom = mm(counts, patch_weights(length, depth)).reshape(SLOTS, SIDE, LANES)

    joined, quads = join(slots.reshape(-1), got, denom)
    joined = joined.reshape(SLOTS, depth * SIDE * SIDE)

    coarse_ids = coarse_target[0, 0]
    owner = coarse_ids // SLOTS
    per_peer = SLOTS // count_x
    number = jnp.arange(SLOTS, dtype=jnp.int32)
    ahead = (owner[:, None] == owner[None, :]) & (number[None, :] < number[:, None])
    coarse_pos = owner * per_peer + jnp.sum(ahead.astype(jnp.int32), axis=1)
    ordering = (coarse_pos[None, :] == number[:, None])
    send_local = jnp.sum(jnp.where(ordering, (coarse_ids % SLOTS)[None, :], 0), axis=1)
    got_local = lax.all_to_all(send_local, "tx", split_axis=0, concat_axis=0, tiled=True)
    flat = quads[:, :, : SIDE // 4].astype(BF16).reshape(SLOTS, -1)
    send_quads = mm(ordering.astype(BF16), flat).astype(BF16)
    got_quads = lax.all_to_all(send_quads, "tx", split_axis=0, concat_axis=0, tiled=True)
    place = (got_local[None, :] == number[:, None]).astype(BF16)
    placed = mm(place, got_quads).reshape(SLOTS, SIDE // 4, SIDE // 4)
    coarse = assemble(placed).astype(BF16)
    return (joined, coarse, corr_right, corr_below)


def solution(mesh):
    placed = (
        P("ty", "tx", None, None, None),
        P("ty", "tx", None),
        P("ty", "tx", None),
        P("ty", "tx", None),
    )
    return jax.shard_map(
        per_device,
        mesh=mesh,
        in_specs=placed,
        out_specs=(P(("ty", "tx"), None), P(("ty", "tx"), None), P("ty", "tx"), P("ty", "tx")),
        check_vma=False,
    )
```

```python
import functools
import math

import jax
import jax.numpy as jnp
from jax import lax
from jax.experimental import pallas as pl
from jax.experimental.pallas import tpu as pltpu
from jax.sharding import PartitionSpec as P

SIDE = 32
OV = 48
H = 8
SLOTS = 64
CODE = 2 * SLOTS
LANES = 128
GROUPS = LANES // SIDE
F32 = jnp.float32
BF16 = jnp.bfloat16


def shifted(value, axis, steps):
    count = lax.axis_size(axis)
    first, last = (max(0, -steps), min(count, count - steps))
    return lax.ppermute(value, axis, [(source, source + steps) for source in range(first, last)])


def highest(left, right):
    return jnp.dot(left, right, precision=lax.Precision.HIGHEST, preferred_element_type=F32)


def iota(shape, dim):
    return lax.broadcasted_iota(jnp.int32, shape, dim)


def mm(a, b):
    return jnp.dot(a, b, preferred_element_type=F32)


def mm_t(a, b):
    return lax.dot_general(a, b, (((1,), (1,)), ((), ())), preferred_element_type=F32)


def bins_kernel(tile_ref, right_ref, left_ref, bottom_ref, top_ref):
    depth, length, _ = tile_ref.shape
    bins = OV // 4
    scale = 1.0 / math.sqrt(16.0 * depth)
    pool = (iota((length, length // 4), 0) // 4 == iota((length, length // 4), 1)).astype(F32)
    first = (iota((16, LANES), 1) // 4 == iota((16, LANES), 0)).astype(BF16)
    last = ((iota((16, LANES), 1) - (LANES - OV)) // 4 == iota((16, LANES), 0)) & (
        iota((16, LANES), 1) >= LANES - OV
    )
    last = last.astype(BF16)
    left = right = top = bottom = jnp.zeros((16, length), F32)
    for z in range(depth):
        left += mm_t(first, tile_ref[z, :, :LANES])
        right += mm_t(last, tile_ref[z, :, length - LANES :])
        top += mm(first, tile_ref[z, :LANES, :])
        bottom += mm(last, tile_ref[z, length - LANES :, :])
    for ref, value in ((right_ref, right), (left_ref, left), (bottom_ref, bottom), (top_ref, top)):
        ref[...] = highest(value, pool)[:bins] * scale


def all_bins(tile):
    length = tile.shape[1]
    shape = jax.ShapeDtypeStruct((OV // 4, length // 4), F32)
    vmem = pl.BlockSpec(memory_space=pltpu.VMEM)
    return pl.pallas_call(
        bins_kernel,
        out_shape=[shape] * 4,
        in_specs=[vmem],
        out_specs=[vmem] * 4,
        name="bins",
        cost_estimate=pl.CostEstimate(flops=10**8, bytes_accessed=2**21, transcendentals=0),
    )(tile)


def dft_tables(length):
    index = jnp.arange(length, dtype=jnp.int32)
    product = index[:, None] * index[None, :] % length
    angle = product.astype(F32) * (2.0 * math.pi / length)
    norm = 1.0 / math.sqrt(length)
    return (jnp.cos(angle) * norm, jnp.sin(angle) * norm)


def phase_kernel(ca_ref, sa_ref, cb_ref, sb_ref, r_ref, l_ref, b_ref, t_ref, right_ref, below_ref):
    cos_a, sin_a, cos_b, sin_b = ca_ref[...], sa_ref[...], cb_ref[...], sb_ref[...]

    def spectrum(values):
        left_cos = highest(cos_a, values)
        left_sin = highest(sin_a, values)
        re = highest(left_cos, cos_b) - highest(left_sin, sin_b)
        im = -(highest(left_cos, sin_b) + highest(left_sin, cos_b))
        return (re, im)

    for own_ref, other_ref, out_ref in ((r_ref, l_ref, right_ref), (b_ref, t_ref, below_ref)):
        own_re, own_im = spectrum(own_ref[...])
        other_re, other_im = spectrum(other_ref[...])
        cross_re = own_re * other_re + own_im * other_im
        cross_im = own_im * other_re - own_re * other_im
        scale = 1.0 / jnp.sqrt(cross_re * cross_re + cross_im * cross_im + 1.0)
        normed_re = cross_re * scale
        normed_im = cross_im * scale
        out = highest(highest(cos_a, normed_re) - highest(sin_a, normed_im), cos_b)
        out = out - highest(highest(sin_a, normed_re) + highest(cos_a, normed_im), sin_b)
        out_ref[...] = out


def phase_surfaces(right, left, bottom, top):
    rows, columns = right.shape
    pad = 16 - rows
    cos_a, sin_a = (jnp.pad(t, ((0, pad), (0, pad))) for t in dft_tables(rows))
    cos_b, sin_b = dft_tables(columns)
    padded = [jnp.pad(v, ((0, pad), (0, 0))) for v in (right, left, bottom, top)]
    vmem = pl.BlockSpec(memory_space=pltpu.VMEM)
    out = pl.pallas_call(
        phase_kernel,
        out_shape=[jax.ShapeDtypeStruct((16, columns), F32)] * 2,
        in_specs=[vmem] * 8,
        out_specs=[vmem] * 2,
        name="phase",
        cost_estimate=pl.CostEstimate(flops=10**8, bytes_accessed=2**18, transcendentals=4096),
    )(cos_a, sin_a, cos_b, sin_b, *padded)
    return out[0][:rows], out[1][:rows]


def swap_groups(parts):
    group = iota(parts[0].shape, 1) // SIDE

    def pick(choices):
        value = choices[3]
        for g in range(3):
            value = jnp.where(group == g, choices[g], value)
        return value

    turned = []
    for d in range(GROUPS):
        mixed = pick([parts[(g + d) % GROUPS] for g in range(GROUPS)])
        turned.append(pltpu.roll(mixed, d * SIDE, 1) if d else mixed)
    return [pick([turned[(j - g) % GROUPS] for j in range(GROUPS)]) for g in range(GROUPS)]


def taps(offset, shape, out_dim, column):
    whole, frac = offset
    at = iota(shape, out_dim) + whole + H
    return (
        jnp.where(column == at, 1.0 - frac, 0.0) + jnp.where(column == at + 1, frac, 0.0)
    ).astype(BF16)


def split_shift(shift):
    whole = lax.shift_right_arithmetic(shift, 2)
    return whole, (shift - 4 * whole).astype(F32) * 0.25


def ramp(shape, dim, length):
    index = iota(shape, dim)
    nearest = jnp.minimum(jnp.minimum(index + 1, length - index), OV).astype(F32)
    return 1.0 + 3.0 * nearest / OV


def pieces_kernel(shift_ref, pos_ref, tile_ref, tb_ref, side_ref, corner_ref, send_ref, work_ref):
    depth, length, _ = tile_ref.shape

    def edge_column(shape, dim):
        c = iota(shape, dim)
        return jnp.where(c < H, c, c + length)

    sy, sx = split_shift(shift_ref[0]), split_shift(shift_ref[1])
    full, thin, wide = (length, length), (length, 2 * H), (2 * H, length)
    ry = taps(sy, full, 0, iota(full, 1) + H)
    ry_edge = taps(sy, thin, 0, edge_column(thin, 1))
    rx = taps(sx, full, 1, iota(full, 0) + H)
    rx_edge = taps(sx, wide, 1, edge_column(wide, 0))
    weights = ramp((length, 1), 0, length) * ramp((1, length), 1, length)
    for z in range(depth):
        along = (mm(ry, tile_ref[z]) + mm(ry_edge, tb_ref[z])).astype(BF16)
        along_side = (mm_t(ry, side_ref[z]) + mm_t(ry_edge, corner_ref[z])).astype(BF16)
        resampled = mm(along, rx) + mm(along_side, rx_edge)
        work_ref[z] = weights * resampled
    send_ref[...] = jnp.zeros_like(send_ref)
    grid_side = length // SIDE

    def row(py, carry):
        start = pl.multiple_of(py * SIDE, SIDE)
        for q in range(length // LANES):
            parts = [work_ref[z, pl.ds(start, SIDE), q * LANES : (q + 1) * LANES] for z in range(depth)]
            for g, piece in enumerate(swap_groups(parts)):
                send_ref[pos_ref[py * grid_side + q * GROUPS + g]] = piece.astype(BF16)
        return carry

    lax.fori_loop(0, grid_side, row, 0)


def make_pieces(shifts, position, tile, tb, side, corner, rows):
    vmem = pl.BlockSpec(memory_space=pltpu.VMEM)
    smem = pl.BlockSpec(memory_space=pltpu.SMEM)
    return pl.pallas_call(
        pieces_kernel,
        out_shape=jax.ShapeDtypeStruct((rows, SIDE, LANES), BF16),
        in_specs=[smem, smem, vmem, vmem, vmem, vmem],
        out_specs=vmem,
        scratch_shapes=[pltpu.VMEM(tile.shape, F32)],
        name="pieces",
        compiler_params=pltpu.CompilerParams(vmem_limit_bytes=40 * 2**20),
        cost_estimate=pl.CostEstimate(flops=2 * 10**9, bytes_accessed=2**23, transcendentals=0),
    )(shifts, position, tile, tb, side, corner)


def join_kernel(slot_ref, got_ref, denom_ref, joined_ref, quads_ref, acc_ref, sum_ref, mean_ref):
    acc_ref[...] = jnp.zeros_like(acc_ref)
    step = 8

    def add(i, carry):
        for j in range(step):
            slot = slot_ref[i * step + j]
            acc_ref[slot] = acc_ref[slot] + got_ref[i * step + j].astype(F32)
        return carry

    lax.fori_loop(0, got_ref.shape[0] // step, add, 0)
    row = iota((LANES, LANES), 0)
    column = iota((LANES, LANES), 1)
    half = SIDE // 2
    pool_one = ((row // (2 * SIDE)) * half + (row % SIDE) // 2 == column).astype(BF16)
    pool_two = (((row % half) // 2 == column) & (row < SIDE)).astype(BF16)
    batch = SLOTS // 4
    rows = batch * SIDE
    for c in range(SLOTS // batch):
        part = pl.ds(c * batch, batch)
        value = (acc_ref[part] / jnp.maximum(denom_ref[part], 1.0)).astype(BF16).reshape(rows, LANES)
        mean_ref[...] = value.astype(F32)
        sum_ref[...] = mm(value, pool_one)
        level = (sum_ref[pl.ds(0, rows // 2, stride=2), :] + sum_ref[pl.ds(1, rows // 2, stride=2), :]) * 0.125
        sum_ref[pl.ds(0, rows // 2), :] = mm(level.astype(BF16), pool_two)
        quads_ref[pl.ds(c * rows // 4, rows // 4), :] = (
            sum_ref[pl.ds(0, rows // 4, stride=2), :] + sum_ref[pl.ds(1, rows // 4, stride=2), :]
        ) * 0.125
        parts = [mean_ref[pl.ds(j, rows // GROUPS, stride=GROUPS), :] for j in range(GROUPS)]
        high = SIDE // GROUPS
        for g, piece in enumerate(swap_groups(parts)):
            joined_ref[part, pl.ds(g * high, high), :] = piece.reshape(batch, high, LANES).astype(BF16)


def join(slots, got, denom):
    vmem = pl.BlockSpec(memory_space=pltpu.VMEM)
    smem = pl.BlockSpec(memory_space=pltpu.SMEM)
    return pl.pallas_call(
        join_kernel,
        out_shape=[
            jax.ShapeDtypeStruct((SLOTS, SIDE, LANES), BF16),
            jax.ShapeDtypeStruct((SLOTS * SIDE // 4, LANES), F32),
        ],
        in_specs=[smem, vmem, vmem],
        out_specs=[vmem, vmem],
        scratch_shapes=[
            pltpu.VMEM((SLOTS + 1, SIDE, LANES), F32),
            pltpu.VMEM((SLOTS // 4 * SIDE, LANES), F32),
            pltpu.VMEM((SLOTS // 4 * SIDE, LANES), F32),
        ],
        name="join",
        compiler_params=pltpu.CompilerParams(vmem_limit_bytes=32 * 2**20),
        cost_estimate=pl.CostEstimate(flops=10**8, bytes_accessed=2**23, transcendentals=0),
    )(slots, got, denom)


def assemble(quadrant_blocks):
    count, height, width = quadrant_blocks.shape
    shaped = quadrant_blocks.reshape(count // 4, 2, 2, height, width).transpose(0, 1, 3, 2, 4)
    return shaped.reshape(count // 4, 4 * height * width)


def patch_weights(length, depth):
    grid_side = length // SIDE
    index = jnp.arange(length, dtype=jnp.int32)
    nearest = jnp.minimum(jnp.minimum(index + 1, length - index), OV).astype(F32)
    line = (1.0 + 3.0 * nearest / OV).reshape(grid_side, SIDE)
    across = jnp.tile(line, (1, depth))
    blend = line[:, None, :, None] * across[None, :, None, :]
    return blend.astype(BF16).reshape(grid_side * grid_side, SIDE * depth * SIDE)


def per_device(tiles, shifts, piece_target, coarse_target):
    tile = tiles[0, 0]
    count_y = lax.axis_size("ty")
    count_x = lax.axis_size("tx")
    devices = count_y * count_x
    depth, length, _ = tile.shape
    pieces_n = (length // SIDE) ** 2
    capacity = 2 * pieces_n // devices

    targets = piece_target[0, 0]
    owners = targets // SLOTS
    order = jnp.arange(pieces_n, dtype=jnp.int32)
    earlier = (owners[:, None] == owners[None, :]) & (order[None, :] < order[:, None])
    position = owners * capacity + jnp.sum(earlier.astype(jnp.int32), axis=1)
    codes = order * CODE + targets % SLOTS - SLOTS
    rows = jnp.arange(devices * capacity, dtype=jnp.int32)
    send_codes = SLOTS + jnp.sum(
        jnp.where(position[None, :] == rows[:, None], codes[None, :], 0), axis=1
    )
    got_codes = lax.all_to_all(send_codes, ("ty", "tx"), split_axis=0, concat_axis=0, tiled=True)

    top = shifted(tile[:, length - H :, :], "ty", 1)
    bottom = shifted(tile[:, :H, :], "ty", -1)
    tb = jnp.concatenate([top, bottom], axis=1)
    last = jnp.concatenate([tile[:, :, length - H :], tb[:, :, length - H :]], axis=1)
    first = jnp.concatenate([tile[:, :, :H], tb[:, :, :H]], axis=1)
    left = shifted(last.transpose(0, 2, 1), "tx", 1)
    right = shifted(first.transpose(0, 2, 1), "tx", -1)
    side = jnp.concatenate([left, right], axis=1)
    right_bins, left_bins, bottom_bins, top_bins = all_bins(tile)
    position, got_codes, left_bins, top_bins = lax.optimization_barrier(
        (position, got_codes, left_bins, top_bins)
    )
    next_left = shifted(left_bins, "tx", -1)
    next_top = shifted(top_bins, "ty", -1)
    send = make_pieces(
        shifts[0, 0], position, tile, tb, side[:, :, :length], side[:, :, length:], devices * capacity
    )
    got = lax.all_to_all(send, ("ty", "tx"), split_axis=0, concat_axis=0, tiled=True)

    corr_right, corr_below = phase_surfaces(right_bins, next_left, bottom_bins, next_top)
    slots = got_codes % CODE
    slot_marks = slots[None, :] == jnp.arange(SLOTS, dtype=jnp.int32)[:, None]
    place_marks = (got_codes // CODE)[:, None] == order[None, :]
    counts = mm(slot_marks.astype(BF16), place_marks.astype(BF16)).astype(BF16)
    denom = mm(counts, patch_weights(length, depth)).reshape(SLOTS, SIDE, LANES)

    coarse_ids = coarse_target[0, 0]
    owner = coarse_ids // SLOTS
    per_peer = SLOTS // count_x
    number = jnp.arange(SLOTS, dtype=jnp.int32)
    ahead = (owner[:, None] == owner[None, :]) & (number[None, :] < number[:, None])
    coarse_pos = owner * per_peer + jnp.sum(ahead.astype(jnp.int32), axis=1)
    ordering = (coarse_pos[None, :] == number[:, None]).astype(BF16)
    locals_ = jnp.broadcast_to((coarse_ids % SLOTS).astype(BF16)[:, None], (SLOTS, SLOTS))
    got, denom, slots, ordering, locals_, corr_right, corr_below = lax.optimization_barrier(
        (got, denom, slots, ordering, locals_, corr_right, corr_below)
    )
    joined, quads = join(slots, got, denom)
    joined = joined.reshape(SLOTS, depth * SIDE * SIDE)
    flat = quads[:, : SIDE // 4].astype(BF16).reshape(SLOTS, -1)
    send_quads = mm(ordering, jnp.concatenate([flat, locals_], axis=1)).astype(BF16)
    got_quads = lax.all_to_all(send_quads, "tx", split_axis=0, concat_axis=0, tiled=True)
    width = flat.shape[1]
    got_local = got_quads[:, width].astype(jnp.int32)
    place = (got_local[None, :] == number[:, None]).astype(BF16)
    placed = mm(place, got_quads[:, :width]).reshape(SLOTS, SIDE // 4, SIDE // 4)
    coarse = assemble(placed).astype(BF16)
    return (joined, coarse, corr_right, corr_below)


def solution(mesh):
    placed = (
        P("ty", "tx", None, None, None),
        P("ty", "tx", None),
        P("ty", "tx", None),
        P("ty", "tx", None),
    )
    return jax.shard_map(
        per_device,
        mesh=mesh,
        in_specs=placed,
        out_specs=(P(("ty", "tx"), None), P(("ty", "tx"), None), P("ty", "tx"), P("ty", "tx")),
        check_vma=False,
    )
```

```python
import functools
import math

import jax
import jax.numpy as jnp
from jax import lax
from jax.experimental import pallas as pl
from jax.experimental.pallas import tpu as pltpu
from jax.sharding import PartitionSpec as P

SIDE = 32
OV = 48
H = 8
SLOTS = 64
CODE = 2 * SLOTS
TX = ("tz", "tw")
PLANE = ("ty", "tw")
PARTS = 2
PART_ROWS = SIDE // PARTS
LANES = 128
GROUPS = LANES // SIDE
F32 = jnp.float32
BF16 = jnp.bfloat16


def shifted(value, axis, steps):
    count = math.prod(lax.axis_size(name) for name in axis)
    first, last = (max(0, -steps), min(count, count - steps))
    return lax.ppermute(value, axis, [(source, source + steps) for source in range(first, last)])


def highest(left, right):
    return jnp.dot(left, right, precision=lax.Precision.HIGHEST, preferred_element_type=F32)


def iota(shape, dim):
    return lax.broadcasted_iota(jnp.int32, shape, dim)


def mm(a, b):
    return jnp.dot(a, b, preferred_element_type=F32)


def mm_t(a, b):
    return lax.dot_general(a, b, (((1,), (1,)), ((), ())), preferred_element_type=F32)


def bins_kernel(tile_ref, right_ref, left_ref, bottom_ref, top_ref):
    depth, length, _ = tile_ref.shape
    bins = OV // 4
    scale = 1.0 / math.sqrt(16.0 * depth)
    pool = (iota((length, length // 4), 0) // 4 == iota((length, length // 4), 1)).astype(F32)
    first = (iota((16, LANES), 1) // 4 == iota((16, LANES), 0)).astype(BF16)
    last = ((iota((16, LANES), 1) - (LANES - OV)) // 4 == iota((16, LANES), 0)) & (
        iota((16, LANES), 1) >= LANES - OV
    )
    last = last.astype(BF16)
    left = right = top = bottom = jnp.zeros((16, length), F32)
    for z in range(depth):
        left += mm_t(first, tile_ref[z, :, :LANES])
        right += mm_t(last, tile_ref[z, :, length - LANES :])
        top += mm(first, tile_ref[z, :LANES, :])
        bottom += mm(last, tile_ref[z, length - LANES :, :])
    for ref, value in ((right_ref, right), (left_ref, left), (bottom_ref, bottom), (top_ref, top)):
        ref[...] = highest(value, pool)[:bins] * scale


def all_bins(tile):
    length = tile.shape[1]
    shape = jax.ShapeDtypeStruct((OV // 4, length // 4), F32)
    vmem = pl.BlockSpec(memory_space=pltpu.VMEM)
    return pl.pallas_call(
        bins_kernel,
        out_shape=[shape] * 4,
        in_specs=[vmem],
        out_specs=[vmem] * 4,
        name="bins",
        cost_estimate=pl.CostEstimate(flops=10**8, bytes_accessed=2**21, transcendentals=0),
    )(tile)


def dft_tables(length):
    index = jnp.arange(length, dtype=jnp.int32)
    product = index[:, None] * index[None, :] % length
    angle = product.astype(F32) * (2.0 * math.pi / length)
    norm = 1.0 / math.sqrt(length)
    return (jnp.cos(angle) * norm, jnp.sin(angle) * norm)


def phase_kernel(ca_ref, sa_ref, cb_ref, sb_ref, r_ref, l_ref, b_ref, t_ref, right_ref, below_ref):
    cos_a, sin_a, cos_b, sin_b = ca_ref[...], sa_ref[...], cb_ref[...], sb_ref[...]

    def spectrum(values):
        left_cos = highest(cos_a, values)
        left_sin = highest(sin_a, values)
        re = highest(left_cos, cos_b) - highest(left_sin, sin_b)
        im = -(highest(left_cos, sin_b) + highest(left_sin, cos_b))
        return (re, im)

    for own_ref, other_ref, out_ref in ((r_ref, l_ref, right_ref), (b_ref, t_ref, below_ref)):
        own_re, own_im = spectrum(own_ref[...])
        other_re, other_im = spectrum(other_ref[...])
        cross_re = own_re * other_re + own_im * other_im
        cross_im = own_im * other_re - own_re * other_im
        scale = 1.0 / jnp.sqrt(cross_re * cross_re + cross_im * cross_im + 1.0)
        normed_re = cross_re * scale
        normed_im = cross_im * scale
        out = highest(highest(cos_a, normed_re) - highest(sin_a, normed_im), cos_b)
        out = out - highest(highest(sin_a, normed_re) + highest(cos_a, normed_im), sin_b)
        out_ref[...] = out


def phase_surfaces(right, left, bottom, top):
    rows, columns = right.shape
    pad = 16 - rows
    cos_a, sin_a = (jnp.pad(t, ((0, pad), (0, pad))) for t in dft_tables(rows))
    cos_b, sin_b = dft_tables(columns)
    padded = [jnp.pad(v, ((0, pad), (0, 0))) for v in (right, left, bottom, top)]
    vmem = pl.BlockSpec(memory_space=pltpu.VMEM)
    out = pl.pallas_call(
        phase_kernel,
        out_shape=[jax.ShapeDtypeStruct((16, columns), F32)] * 2,
        in_specs=[vmem] * 8,
        out_specs=[vmem] * 2,
        name="phase",
        cost_estimate=pl.CostEstimate(flops=10**8, bytes_accessed=2**18, transcendentals=4096),
    )(cos_a, sin_a, cos_b, sin_b, *padded)
    return out[0][:rows], out[1][:rows]


def swap_groups(parts):
    group = iota(parts[0].shape, 1) // SIDE

    def pick(choices):
        value = choices[3]
        for g in range(3):
            value = jnp.where(group == g, choices[g], value)
        return value

    turned = []
    for d in range(GROUPS):
        mixed = pick([parts[(g + d) % GROUPS] for g in range(GROUPS)])
        turned.append(pltpu.roll(mixed, d * SIDE, 1) if d else mixed)
    return [pick([turned[(j - g) % GROUPS] for j in range(GROUPS)]) for g in range(GROUPS)]


def taps(offset, shape, out_dim, column):
    whole, frac = offset
    at = iota(shape, out_dim) + whole + H
    return (
        jnp.where(column == at, 1.0 - frac, 0.0) + jnp.where(column == at + 1, frac, 0.0)
    ).astype(BF16)


def split_shift(shift):
    whole = lax.shift_right_arithmetic(shift, 2)
    return whole, (shift - 4 * whole).astype(F32) * 0.25


def ramp(shape, dim, length):
    index = iota(shape, dim)
    nearest = jnp.minimum(jnp.minimum(index + 1, length - index), OV).astype(F32)
    return 1.0 + 3.0 * nearest / OV


def pieces_kernel(shift_ref, pos_ref, tile_ref, tb_ref, side_ref, corner_ref, *rest):
    send_refs, work_ref = rest[:PARTS], rest[PARTS]
    depth, length, _ = tile_ref.shape

    def edge_column(shape, dim):
        c = iota(shape, dim)
        return jnp.where(c < H, c, c + length)

    sy, sx = split_shift(shift_ref[0]), split_shift(shift_ref[1])
    full, thin, wide = (length, length), (length, 2 * H), (2 * H, length)
    ry = taps(sy, full, 0, iota(full, 1) + H)
    ry_edge = taps(sy, thin, 0, edge_column(thin, 1))
    rx = taps(sx, full, 1, iota(full, 0) + H)
    rx_edge = taps(sx, wide, 1, edge_column(wide, 0))
    weights = ramp((length, 1), 0, length) * ramp((1, length), 1, length)
    for z in range(depth):
        along = (mm(ry, tile_ref[z]) + mm(ry_edge, tb_ref[z])).astype(BF16)
        along_side = (mm_t(ry, side_ref[z]) + mm_t(ry_edge, corner_ref[z])).astype(BF16)
        resampled = mm(along, rx) + mm(along_side, rx_edge)
        work_ref[z] = weights * resampled
    for send_ref in send_refs:
        send_ref[...] = jnp.zeros_like(send_ref)
    grid_side = length // SIDE

    def row(py, carry):
        start = pl.multiple_of(py * SIDE, SIDE)
        for q in range(length // LANES):
            parts = [work_ref[z, pl.ds(start, SIDE), q * LANES : (q + 1) * LANES] for z in range(depth)]
            for g, piece in enumerate(swap_groups(parts)):
                at = pos_ref[py * grid_side + q * GROUPS + g]
                for c, send_ref in enumerate(send_refs):
                    send_ref[at] = piece[c * PART_ROWS : (c + 1) * PART_ROWS].astype(BF16)
        return carry

    lax.fori_loop(0, grid_side, row, 0)


def make_pieces(shifts, position, tile, tb, side, corner, rows):
    vmem = pl.BlockSpec(memory_space=pltpu.VMEM)
    smem = pl.BlockSpec(memory_space=pltpu.SMEM)
    return pl.pallas_call(
        pieces_kernel,
        out_shape=[jax.ShapeDtypeStruct((rows, PART_ROWS, LANES), BF16)] * PARTS,
        in_specs=[smem, smem, vmem, vmem, vmem, vmem],
        out_specs=[vmem] * PARTS,
        scratch_shapes=[pltpu.VMEM(tile.shape, F32)],
        name="pieces",
        compiler_params=pltpu.CompilerParams(vmem_limit_bytes=40 * 2**20),
        cost_estimate=pl.CostEstimate(flops=2 * 10**9, bytes_accessed=2**23, transcendentals=0),
    )(shifts, position, tile, tb, side, corner)


def gather_kernel(slot_ref, got_ref, *rest):
    sum_refs, acc_ref = rest[:-1], rest[-1]
    acc_ref[...] = jnp.zeros_like(acc_ref)
    step = 8

    def add(i, carry):
        for j in range(step):
            slot = slot_ref[i * step + j]
            acc_ref[slot] = acc_ref[slot] + got_ref[i * step + j].astype(F32)
        return carry

    lax.fori_loop(0, got_ref.shape[0] // step, add, 0)
    for z, sum_ref in enumerate(sum_refs):
        sum_ref[...] = acc_ref[pl.ds(z * SLOTS, SLOTS)].astype(BF16)


def gather(slots, got, count):
    vmem = pl.BlockSpec(memory_space=pltpu.VMEM)
    smem = pl.BlockSpec(memory_space=pltpu.SMEM)
    return pl.pallas_call(
        gather_kernel,
        out_shape=[jax.ShapeDtypeStruct((SLOTS,) + got.shape[1:], BF16)] * count,
        in_specs=[smem, vmem],
        out_specs=[vmem] * count,
        scratch_shapes=[pltpu.VMEM((count * SLOTS + 1,) + got.shape[1:], F32)],
        name="gather",
        compiler_params=pltpu.CompilerParams(vmem_limit_bytes=24 * 2**20),
        cost_estimate=pl.CostEstimate(flops=10**7, bytes_accessed=2**22, transcendentals=0),
    )(slots, got)


def join_kernel(*refs):
    got_refs, (denom_ref, joined_ref, quads_ref, sum_ref, mean_ref) = refs[:-5], refs[-5:]
    count = len(got_refs) // PARTS
    row = iota((LANES, LANES), 0)
    column = iota((LANES, LANES), 1)
    half = SIDE // 2
    pool_one = ((row // (2 * SIDE)) * half + (row % SIDE) // 2 == column).astype(BF16)
    pool_two = (((row % half) // 2 == column) & (row < SIDE)).astype(BF16)
    batch = SLOTS // 4
    rows = batch * SIDE
    for c in range(SLOTS // batch):
        part = pl.ds(c * batch, batch)
        numer = []
        for p in range(PARTS):
            total = got_refs[p * count][part].astype(F32)
            for z in range(1, count):
                total += got_refs[p * count + z][part].astype(F32)
            numer.append(total)
        numer = jnp.concatenate(numer, axis=1)
        value = (numer / jnp.maximum(denom_ref[part], 1.0)).astype(BF16).reshape(rows, LANES)
        mean_ref[...] = value.astype(F32)
        sum_ref[...] = mm(value, pool_one)
        level = (sum_ref[pl.ds(0, rows // 2, stride=2), :] + sum_ref[pl.ds(1, rows // 2, stride=2), :]) * 0.125
        sum_ref[pl.ds(0, rows // 2), :] = mm(level.astype(BF16), pool_two)
        quads_ref[pl.ds(c * rows // 4, rows // 4), :] = (
            sum_ref[pl.ds(0, rows // 4, stride=2), :] + sum_ref[pl.ds(1, rows // 4, stride=2), :]
        ) * 0.125
        parts = [mean_ref[pl.ds(j, rows // GROUPS, stride=GROUPS), :] for j in range(GROUPS)]
        high = SIDE // GROUPS
        for g, piece in enumerate(swap_groups(parts)):
            joined_ref[part, pl.ds(g * high, high), :] = piece.reshape(batch, high, LANES).astype(BF16)


def join(got, denom):
    vmem = pl.BlockSpec(memory_space=pltpu.VMEM)
    smem = pl.BlockSpec(memory_space=pltpu.SMEM)
    return pl.pallas_call(
        join_kernel,
        out_shape=[
            jax.ShapeDtypeStruct((SLOTS, SIDE, LANES), BF16),
            jax.ShapeDtypeStruct((SLOTS * SIDE // 4, LANES), F32),
        ],
        in_specs=[vmem] * (len(got) + 1),
        out_specs=[vmem, vmem],
        scratch_shapes=[
            pltpu.VMEM((SLOTS // 4 * SIDE, LANES), F32),
            pltpu.VMEM((SLOTS // 4 * SIDE, LANES), F32),
        ],
        name="join",
        compiler_params=pltpu.CompilerParams(vmem_limit_bytes=32 * 2**20),
        cost_estimate=pl.CostEstimate(flops=10**8, bytes_accessed=2**23, transcendentals=0),
    )(*got, denom)


def assemble(quadrant_blocks):
    count, height, width = quadrant_blocks.shape
    shaped = quadrant_blocks.reshape(count // 4, 2, 2, height, width).transpose(0, 1, 3, 2, 4)
    return shaped.reshape(count // 4, 4 * height * width)


def patch_weights(length, depth):
    grid_side = length // SIDE
    index = jnp.arange(length, dtype=jnp.int32)
    nearest = jnp.minimum(jnp.minimum(index + 1, length - index), OV).astype(F32)
    line = (1.0 + 3.0 * nearest / OV).reshape(grid_side, SIDE)
    across = jnp.tile(line, (1, depth))
    blend = line[:, None, :, None] * across[None, :, None, :]
    return blend.astype(BF16).reshape(grid_side * grid_side, SIDE * depth * SIDE)


def per_device(tiles, shifts, piece_target, coarse_target):
    tile = tiles[0, 0]
    count_y = lax.axis_size("ty")
    count_z = lax.axis_size("tz")
    count_w = lax.axis_size("tw")
    count_x = count_z * count_w
    devices = count_y * count_x
    depth, length, _ = tile.shape
    pieces_n = (length // SIDE) ** 2
    capacity = 2 * pieces_n // devices

    targets = piece_target[0, 0]
    owners = targets // SLOTS
    order = jnp.arange(pieces_n, dtype=jnp.int32)
    earlier = (owners[:, None] == owners[None, :]) & (order[None, :] < order[:, None])
    owner_y, owner_x = owners // count_x, owners % count_x
    owner_z, owner_w = owner_x // count_w, owner_x % count_w
    place = (owner_y * count_w + owner_w) * count_z + owner_z
    position = place * capacity + jnp.sum(earlier.astype(jnp.int32), axis=1)
    codes = order * CODE + targets % SLOTS - SLOTS
    rows = jnp.arange(devices * capacity, dtype=jnp.int32)
    send_codes = SLOTS + jnp.sum(
        jnp.where(position[None, :] == rows[:, None], codes[None, :], 0), axis=1
    )
    got_codes = lax.all_to_all(send_codes, PLANE, split_axis=0, concat_axis=0, tiled=True)

    top = shifted(tile[:, length - H :, :], ("ty",), 1)
    bottom = shifted(tile[:, :H, :], ("ty",), -1)
    tb = jnp.concatenate([top, bottom], axis=1)
    last = jnp.concatenate([tile[:, :, length - H :], tb[:, :, length - H :]], axis=1)
    first = jnp.concatenate([tile[:, :, :H], tb[:, :, :H]], axis=1)
    left = shifted(last.transpose(0, 2, 1), TX, 1)
    right = shifted(first.transpose(0, 2, 1), TX, -1)
    side = jnp.concatenate([left, right], axis=1)
    right_bins, left_bins, bottom_bins, top_bins = all_bins(tile)
    position, got_codes, left_bins, top_bins = lax.optimization_barrier(
        (position, got_codes, left_bins, top_bins)
    )
    next_left = shifted(left_bins, TX, -1)
    next_top = shifted(top_bins, ("ty",), -1)
    send = make_pieces(
        shifts[0, 0], position, tile, tb, side[:, :, :length], side[:, :, length:], devices * capacity
    )
    got = [lax.all_to_all(part, PLANE, split_axis=0, concat_axis=0, tiled=True) for part in send]

    me_z = lax.axis_index("tz")
    slots = got_codes % CODE
    turn = (rows // capacity - me_z) % count_z
    dense = count_z * SLOTS
    slots = jnp.where(slots < SLOTS, turn * SLOTS + slots, dense)

    def turned(values):
        ring = range(count_z)
        return [values[0]] + [
            lax.ppermute(values[r], "tz", [(z, (z + r) % count_z) for z in ring]) for r in ring[1:]
        ]

    sums = [value for part in got for value in turned(gather(slots, part, count_z))]

    corr_right, corr_below = phase_surfaces(right_bins, next_left, bottom_bins, next_top)
    slot_marks = slots[None, :] == jnp.arange(dense, dtype=jnp.int32)[:, None]
    place_marks = (got_codes // CODE)[:, None] == order[None, :]
    counts = mm(slot_marks.astype(BF16), place_marks.astype(BF16)).astype(BF16)
    counts = turned(list(counts.reshape(count_z, SLOTS, -1)))
    counts = sum(value.astype(F32) for value in counts).astype(BF16)
    denom = mm(counts, patch_weights(length, depth)).reshape(SLOTS, SIDE, LANES)

    coarse_ids = coarse_target[0, 0]
    owner = coarse_ids // SLOTS
    per_peer = SLOTS // count_x
    number = jnp.arange(SLOTS, dtype=jnp.int32)
    ahead = (owner[:, None] == owner[None, :]) & (number[None, :] < number[:, None])
    coarse_pos = owner * per_peer + jnp.sum(ahead.astype(jnp.int32), axis=1)
    ordering = (coarse_pos[None, :] == number[:, None]).astype(BF16)
    locals_ = jnp.broadcast_to((coarse_ids % SLOTS).astype(BF16)[:, None], (SLOTS, SLOTS))
    sums, denom, ordering, locals_, corr_right, corr_below = lax.optimization_barrier(
        (sums, denom, ordering, locals_, corr_right, corr_below)
    )
    joined, quads = join(sums, denom)
    joined = joined.reshape(SLOTS, depth * SIDE * SIDE)
    flat = quads[:, : SIDE // 4].astype(BF16).reshape(SLOTS, -1)
    send_quads = mm(ordering, jnp.concatenate([flat, locals_], axis=1)).astype(BF16)
    got_quads = lax.all_to_all(send_quads, TX, split_axis=0, concat_axis=0, tiled=True)
    width = flat.shape[1]
    got_local = got_quads[:, width].astype(jnp.int32)
    place = (got_local[None, :] == number[:, None]).astype(BF16)
    placed = mm(place, got_quads[:, :width]).reshape(SLOTS, SIDE // 4, SIDE // 4)
    coarse = assemble(placed).astype(BF16)
    return (joined, coarse, corr_right, corr_below)


def solution(mesh):
    count_y, count_x = mesh.devices.shape
    count_z = math.gcd(count_x, 4)
    split = jax.sharding.Mesh(
        mesh.devices.reshape(count_y, count_z, count_x // count_z), ("ty", "tz", "tw")
    )
    placed = (P("ty", TX, None, None, None), P("ty", TX, None), P("ty", TX, None), P("ty", TX, None))
    every = ("ty",) + TX
    return jax.shard_map(
        per_device,
        mesh=split,
        in_specs=placed,
        out_specs=(P(every, None), P(every, None), P("ty", TX), P("ty", TX)),
        check_vma=False,
    )
```

```python
import functools
import math

import jax
import jax.numpy as jnp
from jax import lax
from jax.experimental import pallas as pl
from jax.experimental.pallas import tpu as pltpu
from jax.sharding import PartitionSpec as P

SIDE = 32
OV = 48
H = 8
SLOTS = 64
CODE = 2 * SLOTS
LANES = 128
GROUPS = LANES // SIDE
F32 = jnp.float32
BF16 = jnp.bfloat16


def shifted(value, axis, steps):
    count = lax.axis_size(axis)
    first, last = (max(0, -steps), min(count, count - steps))
    return lax.ppermute(value, axis, [(source, source + steps) for source in range(first, last)])


def highest(left, right):
    return jnp.dot(left, right, precision=lax.Precision.HIGHEST, preferred_element_type=F32)


def iota(shape, dim):
    return lax.broadcasted_iota(jnp.int32, shape, dim)


def mm(a, b):
    return jnp.dot(a, b, preferred_element_type=F32)


def mm_t(a, b):
    return lax.dot_general(a, b, (((1,), (1,)), ((), ())), preferred_element_type=F32)


def bins_kernel(tile_ref, right_ref, left_ref, bottom_ref, top_ref):
    depth, length, _ = tile_ref.shape
    bins = OV // 4
    scale = 1.0 / math.sqrt(16.0 * depth)
    pool = (iota((length, length // 4), 0) // 4 == iota((length, length // 4), 1)).astype(F32)
    first = (iota((16, LANES), 1) // 4 == iota((16, LANES), 0)).astype(BF16)
    last = ((iota((16, LANES), 1) - (LANES - OV)) // 4 == iota((16, LANES), 0)) & (
        iota((16, LANES), 1) >= LANES - OV
    )
    last = last.astype(BF16)
    left = right = top = bottom = jnp.zeros((16, length), F32)
    for z in range(depth):
        left += mm_t(first, tile_ref[z, :, :LANES])
        right += mm_t(last, tile_ref[z, :, length - LANES :])
        top += mm(first, tile_ref[z, :LANES, :])
        bottom += mm(last, tile_ref[z, length - LANES :, :])
    for ref, value in ((right_ref, right), (left_ref, left), (bottom_ref, bottom), (top_ref, top)):
        ref[...] = highest(value, pool)[:bins] * scale


def all_bins(tile):
    length = tile.shape[1]
    shape = jax.ShapeDtypeStruct((OV // 4, length // 4), F32)
    vmem = pl.BlockSpec(memory_space=pltpu.VMEM)
    return pl.pallas_call(
        bins_kernel,
        out_shape=[shape] * 4,
        in_specs=[vmem],
        out_specs=[vmem] * 4,
        name="bins",
        cost_estimate=pl.CostEstimate(flops=10**8, bytes_accessed=2**21, transcendentals=0),
    )(tile)


def dft_tables(length):
    index = jnp.arange(length, dtype=jnp.int32)
    product = index[:, None] * index[None, :] % length
    angle = product.astype(F32) * (2.0 * math.pi / length)
    norm = 1.0 / math.sqrt(length)
    return (jnp.cos(angle) * norm, jnp.sin(angle) * norm)


def phase_kernel(ca_ref, sa_ref, cb_ref, sb_ref, r_ref, l_ref, b_ref, t_ref, right_ref, below_ref):
    cos_a, sin_a, cos_b, sin_b = ca_ref[...], sa_ref[...], cb_ref[...], sb_ref[...]

    def spectrum(values):
        left_cos = highest(cos_a, values)
        left_sin = highest(sin_a, values)
        re = highest(left_cos, cos_b) - highest(left_sin, sin_b)
        im = -(highest(left_cos, sin_b) + highest(left_sin, cos_b))
        return (re, im)

    for own_ref, other_ref, out_ref in ((r_ref, l_ref, right_ref), (b_ref, t_ref, below_ref)):
        own_re, own_im = spectrum(own_ref[...])
        other_re, other_im = spectrum(other_ref[...])
        cross_re = own_re * other_re + own_im * other_im
        cross_im = own_im * other_re - own_re * other_im
        scale = 1.0 / jnp.sqrt(cross_re * cross_re + cross_im * cross_im + 1.0)
        normed_re = cross_re * scale
        normed_im = cross_im * scale
        out = highest(highest(cos_a, normed_re) - highest(sin_a, normed_im), cos_b)
        out = out - highest(highest(sin_a, normed_re) + highest(cos_a, normed_im), sin_b)
        out_ref[...] = out


def phase_surfaces(right, left, bottom, top):
    rows, columns = right.shape
    pad = 16 - rows
    cos_a, sin_a = (jnp.pad(t, ((0, pad), (0, pad))) for t in dft_tables(rows))
    cos_b, sin_b = dft_tables(columns)
    padded = [jnp.pad(v, ((0, pad), (0, 0))) for v in (right, left, bottom, top)]
    vmem = pl.BlockSpec(memory_space=pltpu.VMEM)
    out = pl.pallas_call(
        phase_kernel,
        out_shape=[jax.ShapeDtypeStruct((16, columns), F32)] * 2,
        in_specs=[vmem] * 8,
        out_specs=[vmem] * 2,
        name="phase",
        cost_estimate=pl.CostEstimate(flops=10**8, bytes_accessed=2**18, transcendentals=4096),
    )(cos_a, sin_a, cos_b, sin_b, *padded)
    return out[0][:rows], out[1][:rows]


def swap_groups(parts):
    group = iota(parts[0].shape, 1) // SIDE

    def pick(choices):
        value = choices[3]
        for g in range(3):
            value = jnp.where(group == g, choices[g], value)
        return value

    turned = []
    for d in range(GROUPS):
        mixed = pick([parts[(g + d) % GROUPS] for g in range(GROUPS)])
        turned.append(pltpu.roll(mixed, d * SIDE, 1) if d else mixed)
    return [pick([turned[(j - g) % GROUPS] for j in range(GROUPS)]) for g in range(GROUPS)]


def taps(offset, shape, out_dim, column):
    whole, frac = offset
    at = iota(shape, out_dim) + whole + H
    return (
        jnp.where(column == at, 1.0 - frac, 0.0) + jnp.where(column == at + 1, frac, 0.0)
    ).astype(BF16)


def split_shift(shift):
    whole = lax.shift_right_arithmetic(shift, 2)
    return whole, (shift - 4 * whole).astype(F32) * 0.25


def ramp(shape, dim, length):
    index = iota(shape, dim)
    nearest = jnp.minimum(jnp.minimum(index + 1, length - index), OV).astype(F32)
    return 1.0 + 3.0 * nearest / OV


def pieces_kernel(shift_ref, pos_ref, tile_ref, tb_ref, side_ref, corner_ref, send_ref, work_ref):
    depth, length, _ = tile_ref.shape

    def edge_column(shape, dim):
        c = iota(shape, dim)
        return jnp.where(c < H, c, c + length)

    sy, sx = split_shift(shift_ref[0]), split_shift(shift_ref[1])
    full, thin, wide = (length, length), (length, 2 * H), (2 * H, length)
    ry = taps(sy, full, 0, iota(full, 1) + H)
    ry_edge = taps(sy, thin, 0, edge_column(thin, 1))
    rx = taps(sx, full, 1, iota(full, 0) + H)
    rx_edge = taps(sx, wide, 1, edge_column(wide, 0))
    weights = ramp((length, 1), 0, length) * ramp((1, length), 1, length)
    for z in range(depth):
        along = (mm(ry, tile_ref[z]) + mm(ry_edge, tb_ref[z])).astype(BF16)
        along_side = (mm_t(ry, side_ref[z]) + mm_t(ry_edge, corner_ref[z])).astype(BF16)
        resampled = mm(along, rx) + mm(along_side, rx_edge)
        work_ref[z] = weights * resampled
    send_ref[...] = jnp.zeros_like(send_ref)
    grid_side = length // SIDE

    def row(py, carry):
        start = pl.multiple_of(py * SIDE, SIDE)
        for q in range(length // LANES):
            parts = [work_ref[z, pl.ds(start, SIDE), q * LANES : (q + 1) * LANES] for z in range(depth)]
            for g, piece in enumerate(swap_groups(parts)):
                send_ref[pos_ref[py * grid_side + q * GROUPS + g]] = piece.astype(BF16)
        return carry

    lax.fori_loop(0, grid_side, row, 0)


def make_pieces(shifts, position, tile, tb, side, corner, rows):
    vmem = pl.BlockSpec(memory_space=pltpu.VMEM)
    smem = pl.BlockSpec(memory_space=pltpu.SMEM)
    return pl.pallas_call(
        pieces_kernel,
        out_shape=jax.ShapeDtypeStruct((rows, SIDE, LANES), BF16),
        in_specs=[smem, smem, vmem, vmem, vmem, vmem],
        out_specs=vmem,
        scratch_shapes=[pltpu.VMEM(tile.shape, F32)],
        name="pieces",
        compiler_params=pltpu.CompilerParams(vmem_limit_bytes=40 * 2**20),
        cost_estimate=pl.CostEstimate(flops=2 * 10**9, bytes_accessed=2**23, transcendentals=0),
    )(shifts, position, tile, tb, side, corner)


def exchange_kernel(count_y, count_x, send_ref, code_ref, got_ref, got_code_ref, sems, code_sems, own_sems):
    devices = count_y * count_x
    capacity = send_ref.shape[0] // devices
    me = lax.axis_index("ty") * count_x + lax.axis_index("tx")
    barrier = pltpu.get_barrier_semaphore()

    def at(peer):
        return (peer // count_x, peer % count_x)

    def greet(d, carry):
        pl.semaphore_signal(
            barrier, inc=1, device_id=at((me + d) % devices), device_id_type=pl.DeviceIdType.MESH
        )
        return carry

    lax.fori_loop(1, devices, greet, 0)
    pl.semaphore_wait(barrier, devices - 1)

    def copies(source, target, peer):
        block = pl.ds(source * capacity, capacity)
        landing = pl.ds(target * capacity, capacity)
        pieces = pltpu.make_async_remote_copy(
            src_ref=send_ref.at[block],
            dst_ref=got_ref.at[landing],
            send_sem=sems.at[0, source],
            recv_sem=sems.at[1, target],
            device_id=at(peer),
            device_id_type=pl.DeviceIdType.MESH,
        )
        codes = pltpu.make_async_remote_copy(
            src_ref=code_ref.at[source],
            dst_ref=got_code_ref.at[target],
            send_sem=code_sems.at[0, source],
            recv_sem=code_sems.at[1, target],
            device_id=at(peer),
            device_id_type=pl.DeviceIdType.MESH,
        )
        return pieces, codes

    def start(d, carry):
        peer = (me + d) % devices
        for copy in copies(peer, me, peer):
            copy.start()
        return carry

    lax.fori_loop(1, devices, start, 0)
    mine = pl.ds(me * capacity, capacity)
    own = pltpu.make_async_copy(send_ref.at[mine], got_ref.at[mine], own_sems.at[0])
    own_code = pltpu.make_async_copy(code_ref.at[me], got_code_ref.at[me], own_sems.at[1])
    own.start()
    own_code.start()
    own.wait()
    own_code.wait()

    def finish(d, carry):
        peer = (me + d) % devices
        for copy in copies(peer, peer, peer):
            copy.wait_send()
            copy.wait_recv()
        return carry

    lax.fori_loop(1, devices, finish, 0)


def exchange(send, codes, count_y, count_x):
    devices = count_y * count_x
    vmem = pl.BlockSpec(memory_space=pltpu.VMEM)
    return pl.pallas_call(
        functools.partial(exchange_kernel, count_y, count_x),
        out_shape=[
            jax.ShapeDtypeStruct(send.shape, send.dtype),
            jax.ShapeDtypeStruct(codes.shape, codes.dtype),
        ],
        in_specs=[vmem, vmem],
        out_specs=[vmem, vmem],
        scratch_shapes=[
            pltpu.SemaphoreType.DMA((2, devices)),
            pltpu.SemaphoreType.DMA((2, devices)),
            pltpu.SemaphoreType.DMA((2,)),
        ],
        name="exchange",
        compiler_params=pltpu.CompilerParams(
            collective_id=0, has_side_effects=True, vmem_limit_bytes=24 * 2**20
        ),
        cost_estimate=pl.CostEstimate(flops=0, bytes_accessed=2**23, transcendentals=0),
    )(send, codes)


def join_kernel(slot_ref, code_ref, patch_ref, got_ref, joined_ref, quads_ref, acc_ref, sum_ref, mean_ref, denom_ref):
    acc_ref[...] = jnp.zeros_like(acc_ref)
    step = 8

    def add(i, carry):
        for j in range(step):
            slot = slot_ref[i * step + j]
            acc_ref[slot] = acc_ref[slot] + got_ref[i * step + j].astype(F32)
        return carry

    lax.fori_loop(0, got_ref.shape[0] // step, add, 0)
    codes = code_ref[...]
    number = codes.shape[1]
    grid = patch_ref.shape[1]
    slot_marks = (codes % CODE == iota((SLOTS, number), 0)).astype(BF16)
    place_marks = (codes // CODE == iota((grid, number), 0)).astype(BF16)
    counts = mm_t(slot_marks, place_marks).astype(BF16)
    for y in range(SIDE):
        denom_ref[pl.ds(y, SLOTS, stride=SIDE), :] = mm(counts, patch_ref[y])
    row = iota((LANES, LANES), 0)
    column = iota((LANES, LANES), 1)
    half = SIDE // 2
    pool_one = ((row // (2 * SIDE)) * half + (row % SIDE) // 2 == column).astype(BF16)
    pool_two = (((row % half) // 2 == column) & (row < SIDE)).astype(BF16)
    batch = SLOTS // 4
    rows = batch * SIDE
    for c in range(SLOTS // batch):
        part = pl.ds(c * batch, batch)
        denom = jnp.maximum(denom_ref[pl.ds(c * rows, rows), :], 1.0)
        value = (acc_ref[part].reshape(rows, LANES) / denom).astype(BF16)
        mean_ref[...] = value.astype(F32)
        sum_ref[...] = mm(value, pool_one)
        level = (sum_ref[pl.ds(0, rows // 2, stride=2), :] + sum_ref[pl.ds(1, rows // 2, stride=2), :]) * 0.125
        sum_ref[pl.ds(0, rows // 2), :] = mm(level.astype(BF16), pool_two)
        quads_ref[pl.ds(c * rows // 4, rows // 4), :] = (
            sum_ref[pl.ds(0, rows // 4, stride=2), :] + sum_ref[pl.ds(1, rows // 4, stride=2), :]
        ) * 0.125
        parts = [mean_ref[pl.ds(j, rows // GROUPS, stride=GROUPS), :] for j in range(GROUPS)]
        high = SIDE // GROUPS
        for g, piece in enumerate(swap_groups(parts)):
            joined_ref[part, pl.ds(g * high, high), :] = piece.reshape(batch, high, LANES).astype(BF16)


def join(slots, codes, patches, got):
    vmem = pl.BlockSpec(memory_space=pltpu.VMEM)
    smem = pl.BlockSpec(memory_space=pltpu.SMEM)
    return pl.pallas_call(
        join_kernel,
        out_shape=[
            jax.ShapeDtypeStruct((SLOTS, SIDE, LANES), BF16),
            jax.ShapeDtypeStruct((SLOTS * SIDE // 4, LANES), F32),
        ],
        in_specs=[smem, vmem, vmem, vmem],
        out_specs=[vmem, vmem],
        scratch_shapes=[
            pltpu.VMEM((SLOTS + 1, SIDE, LANES), F32),
            pltpu.VMEM((SLOTS // 4 * SIDE, LANES), F32),
            pltpu.VMEM((SLOTS // 4 * SIDE, LANES), F32),
            pltpu.VMEM((SLOTS * SIDE, LANES), F32),
        ],
        name="join",
        compiler_params=pltpu.CompilerParams(vmem_limit_bytes=32 * 2**20),
        cost_estimate=pl.CostEstimate(flops=10**8, bytes_accessed=2**23, transcendentals=0),
    )(slots, codes, patches, got)


def assemble(quadrant_blocks):
    count, height, width = quadrant_blocks.shape
    shaped = quadrant_blocks.reshape(count // 4, 2, 2, height, width).transpose(0, 1, 3, 2, 4)
    return shaped.reshape(count // 4, 4 * height * width)


def patch_weights(length, depth):
    grid_side = length // SIDE
    ramps = ramp((1, length), 1, length).reshape(grid_side, SIDE)
    down = jnp.repeat(ramps, grid_side, axis=0).T
    across = jnp.tile(ramps, (grid_side, depth))
    return (down[:, :, None] * across[None]).astype(BF16)


def per_device(tiles, shifts, piece_target, coarse_target):
    tile = tiles[0, 0]
    count_y = lax.axis_size("ty")
    count_x = lax.axis_size("tx")
    devices = count_y * count_x
    depth, length, _ = tile.shape
    pieces_n = (length // SIDE) ** 2
    capacity = 2 * pieces_n // devices

    targets = piece_target[0, 0]
    owners = targets // SLOTS
    order = jnp.arange(pieces_n, dtype=jnp.int32)
    earlier = (owners[:, None] == owners[None, :]) & (order[None, :] < order[:, None])
    position = owners * capacity + jnp.sum(earlier.astype(jnp.int32), axis=1)
    codes = order * CODE + targets % SLOTS - SLOTS
    rows = jnp.arange(devices * capacity, dtype=jnp.int32)
    send_codes = SLOTS + jnp.sum(
        jnp.where(position[None, :] == rows[:, None], codes[None, :], 0), axis=1
    )
    send_codes = jnp.broadcast_to(send_codes.reshape(devices, 1, capacity), (devices, 8, capacity))
    send_codes = jnp.pad(send_codes, ((0, 0), (0, 0), (0, LANES - capacity)))

    top = shifted(tile[:, length - H :, :], "ty", 1)
    bottom = shifted(tile[:, :H, :], "ty", -1)
    tb = jnp.concatenate([top, bottom], axis=1)
    last = jnp.concatenate([tile[:, :, length - H :], tb[:, :, length - H :]], axis=1)
    first = jnp.concatenate([tile[:, :, :H], tb[:, :, :H]], axis=1)
    left = shifted(last.transpose(0, 2, 1), "tx", 1)
    right = shifted(first.transpose(0, 2, 1), "tx", -1)
    side = jnp.concatenate([left, right], axis=1)
    right_bins, left_bins, bottom_bins, top_bins = all_bins(tile)
    next_left = shifted(left_bins, "tx", -1)
    next_top = shifted(top_bins, "ty", -1)
    send = make_pieces(
        shifts[0, 0], position, tile, tb, side[:, :, :length], side[:, :, length:], devices * capacity
    )
    corr_right, corr_below = phase_surfaces(right_bins, next_left, bottom_bins, next_top)
    patches = patch_weights(length, depth)
    got, got_codes = exchange(send, send_codes, count_y, count_x)
    codes = got_codes[:, 0, :capacity].reshape(-1)

    coarse_ids = coarse_target[0, 0]
    owner = coarse_ids // SLOTS
    per_peer = SLOTS // count_x
    number = jnp.arange(SLOTS, dtype=jnp.int32)
    ahead = (owner[:, None] == owner[None, :]) & (number[None, :] < number[:, None])
    coarse_pos = owner * per_peer + jnp.sum(ahead.astype(jnp.int32), axis=1)
    ordering = (coarse_pos[None, :] == number[:, None]).astype(BF16)
    locals_ = jnp.broadcast_to((coarse_ids % SLOTS).astype(BF16)[:, None], (SLOTS, SLOTS))
    joined, quads = join(codes % CODE, codes[None, :], patches, got)
    joined = joined.reshape(SLOTS, depth * SIDE * SIDE)
    flat = quads[:, : SIDE // 4].astype(BF16).reshape(SLOTS, -1)
    send_quads = mm(ordering, jnp.concatenate([flat, locals_], axis=1)).astype(BF16)
    got_quads = lax.all_to_all(send_quads, "tx", split_axis=0, concat_axis=0, tiled=True)
    width = flat.shape[1]
    got_local = got_quads[:, width].astype(jnp.int32)
    place = (got_local[None, :] == number[:, None]).astype(BF16)
    placed = mm(place, got_quads[:, :width]).reshape(SLOTS, SIDE // 4, SIDE // 4)
    coarse = assemble(placed).astype(BF16)
    return (joined, coarse, corr_right, corr_below)


def solution(mesh):
    placed = (
        P("ty", "tx", None, None, None),
        P("ty", "tx", None),
        P("ty", "tx", None),
        P("ty", "tx", None),
    )
    return jax.shard_map(
        per_device,
        mesh=mesh,
        in_specs=placed,
        out_specs=(P(("ty", "tx"), None), P(("ty", "tx"), None), P("ty", "tx"), P("ty", "tx")),
        check_vma=False,
    )
```

```python
import functools
import math

import jax
import jax.numpy as jnp
from jax import lax
from jax.experimental import pallas as pl
from jax.experimental.pallas import tpu as pltpu
from jax.sharding import PartitionSpec as P

SIDE = 32
OV = 48
H = 8
SLOTS = 64
CODE = 2 * SLOTS
LANES = 128
GROUPS = LANES // SIDE
F32 = jnp.float32
BF16 = jnp.bfloat16


def shifted(value, axis, steps):
    count = lax.axis_size(axis)
    first, last = (max(0, -steps), min(count, count - steps))
    return lax.ppermute(value, axis, [(source, source + steps) for source in range(first, last)])


def highest(left, right):
    return jnp.dot(left, right, precision=lax.Precision.HIGHEST, preferred_element_type=F32)


def iota(shape, dim):
    return lax.broadcasted_iota(jnp.int32, shape, dim)


def mm(a, b):
    return jnp.dot(a, b, preferred_element_type=F32)


def mm_t(a, b):
    return lax.dot_general(a, b, (((1,), (1,)), ((), ())), preferred_element_type=F32)


def bins_kernel(tile_ref, after_ref, right_ref, left_ref, bottom_ref, top_ref):
    depth, length, _ = tile_ref.shape
    bins = OV // 4
    scale = 1.0 / math.sqrt(16.0 * depth)
    pool = (iota((length, length // 4), 0) // 4 == iota((length, length // 4), 1)).astype(F32)
    first = (iota((16, LANES), 1) // 4 == iota((16, LANES), 0)).astype(BF16)
    last = ((iota((16, LANES), 1) - (LANES - OV)) // 4 == iota((16, LANES), 0)) & (
        iota((16, LANES), 1) >= LANES - OV
    )
    last = last.astype(BF16)
    left = right = top = bottom = jnp.zeros((16, length), F32)
    for z in range(depth):
        left += mm_t(first, tile_ref[z, :, :LANES])
        right += mm_t(last, tile_ref[z, :, length - LANES :])
        top += mm(first, tile_ref[z, :LANES, :])
        bottom += mm(last, tile_ref[z, length - LANES :, :])
    for ref, value in ((right_ref, right), (left_ref, left), (bottom_ref, bottom), (top_ref, top)):
        ref[...] = highest(value, pool)[:bins] * scale


def all_bins(tile, after):
    length = tile.shape[1]
    shape = jax.ShapeDtypeStruct((OV // 4, length // 4), F32)
    vmem = pl.BlockSpec(memory_space=pltpu.VMEM)
    return pl.pallas_call(
        bins_kernel,
        out_shape=[shape] * 4,
        in_specs=[vmem, vmem],
        out_specs=[vmem] * 4,
        name="bins",
        cost_estimate=pl.CostEstimate(flops=10**8, bytes_accessed=2**21, transcendentals=0),
    )(tile, after)


def dft_tables(length):
    index = jnp.arange(length, dtype=jnp.int32)
    product = index[:, None] * index[None, :] % length
    angle = product.astype(F32) * (2.0 * math.pi / length)
    norm = 1.0 / math.sqrt(length)
    return (jnp.cos(angle) * norm, jnp.sin(angle) * norm)


def phase_kernel(ca_ref, sa_ref, cb_ref, sb_ref, r_ref, l_ref, b_ref, t_ref, right_ref, below_ref):
    cos_a, sin_a, cos_b, sin_b = ca_ref[...], sa_ref[...], cb_ref[...], sb_ref[...]

    def spectrum(values):
        left_cos = highest(cos_a, values)
        left_sin = highest(sin_a, values)
        re = highest(left_cos, cos_b) - highest(left_sin, sin_b)
        im = -(highest(left_cos, sin_b) + highest(left_sin, cos_b))
        return (re, im)

    for own_ref, other_ref, out_ref in ((r_ref, l_ref, right_ref), (b_ref, t_ref, below_ref)):
        own_re, own_im = spectrum(own_ref[...])
        other_re, other_im = spectrum(other_ref[...])
        cross_re = own_re * other_re + own_im * other_im
        cross_im = own_im * other_re - own_re * other_im
        scale = 1.0 / jnp.sqrt(cross_re * cross_re + cross_im * cross_im + 1.0)
        normed_re = cross_re * scale
        normed_im = cross_im * scale
        out = highest(highest(cos_a, normed_re) - highest(sin_a, normed_im), cos_b)
        out = out - highest(highest(sin_a, normed_re) + highest(cos_a, normed_im), sin_b)
        out_ref[...] = out


def phase_surfaces(right, left, bottom, top):
    rows, columns = right.shape
    pad = 16 - rows
    cos_a, sin_a = (jnp.pad(t, ((0, pad), (0, pad))) for t in dft_tables(rows))
    cos_b, sin_b = dft_tables(columns)
    padded = [jnp.pad(v, ((0, pad), (0, 0))) for v in (right, left, bottom, top)]
    vmem = pl.BlockSpec(memory_space=pltpu.VMEM)
    out = pl.pallas_call(
        phase_kernel,
        out_shape=[jax.ShapeDtypeStruct((16, columns), F32)] * 2,
        in_specs=[vmem] * 8,
        out_specs=[vmem] * 2,
        name="phase",
        cost_estimate=pl.CostEstimate(flops=10**8, bytes_accessed=2**18, transcendentals=4096),
    )(cos_a, sin_a, cos_b, sin_b, *padded)
    return out[0][:rows], out[1][:rows]


def swap_groups(parts):
    group = iota(parts[0].shape, 1) // SIDE

    def pick(choices):
        value = choices[3]
        for g in range(3):
            value = jnp.where(group == g, choices[g], value)
        return value

    turned = []
    for d in range(GROUPS):
        mixed = pick([parts[(g + d) % GROUPS] for g in range(GROUPS)])
        turned.append(pltpu.roll(mixed, d * SIDE, 1) if d else mixed)
    return [pick([turned[(j - g) % GROUPS] for j in range(GROUPS)]) for g in range(GROUPS)]


def taps(offset, shape, out_dim, column):
    whole, frac = offset
    at = iota(shape, out_dim) + whole + H
    return (
        jnp.where(column == at, 1.0 - frac, 0.0) + jnp.where(column == at + 1, frac, 0.0)
    ).astype(BF16)


def split_shift(shift):
    whole = lax.shift_right_arithmetic(shift, 2)
    return whole, (shift - 4 * whole).astype(F32) * 0.25


def ramp(shape, dim, length):
    index = iota(shape, dim)
    nearest = jnp.minimum(jnp.minimum(index + 1, length - index), OV).astype(F32)
    return 1.0 + 3.0 * nearest / OV


def pieces_kernel(shift_ref, pos_ref, tile_ref, tb_ref, side_ref, corner_ref, send_ref, work_ref):
    depth, length, _ = tile_ref.shape

    def edge_column(shape, dim):
        c = iota(shape, dim)
        return jnp.where(c < H, c, c + length)

    sy, sx = split_shift(shift_ref[0]), split_shift(shift_ref[1])
    full, thin, wide = (length, length), (length, 2 * H), (2 * H, length)
    ry = taps(sy, full, 0, iota(full, 1) + H)
    ry_edge = taps(sy, thin, 0, edge_column(thin, 1))
    rx = taps(sx, full, 1, iota(full, 0) + H)
    rx_edge = taps(sx, wide, 1, edge_column(wide, 0))
    weights = ramp((length, 1), 0, length) * ramp((1, length), 1, length)
    for z in range(depth):
        along = (mm(ry, tile_ref[z]) + mm(ry_edge, tb_ref[z])).astype(BF16)
        along_side = (mm_t(ry, side_ref[z]) + mm_t(ry_edge, corner_ref[z])).astype(BF16)
        resampled = mm(along, rx) + mm(along_side, rx_edge)
        work_ref[z] = weights * resampled
    send_ref[...] = jnp.zeros_like(send_ref)
    grid_side = length // SIDE

    def row(py, carry):
        start = pl.multiple_of(py * SIDE, SIDE)
        for q in range(length // LANES):
            parts = [work_ref[z, pl.ds(start, SIDE), q * LANES : (q + 1) * LANES] for z in range(depth)]
            for g, piece in enumerate(swap_groups(parts)):
                send_ref[pos_ref[py * grid_side + q * GROUPS + g]] = piece.astype(BF16)
        return carry

    lax.fori_loop(0, grid_side, row, 0)


def make_pieces(shifts, position, tile, tb, side, corner, rows):
    vmem = pl.BlockSpec(memory_space=pltpu.VMEM)
    smem = pl.BlockSpec(memory_space=pltpu.SMEM)
    return pl.pallas_call(
        pieces_kernel,
        out_shape=jax.ShapeDtypeStruct((rows, SIDE, LANES), BF16),
        in_specs=[smem, smem, vmem, vmem, vmem, vmem],
        out_specs=vmem,
        scratch_shapes=[pltpu.VMEM(tile.shape, F32)],
        name="pieces",
        compiler_params=pltpu.CompilerParams(vmem_limit_bytes=24 * 2**20),
        cost_estimate=pl.CostEstimate(flops=2 * 10**9, bytes_accessed=2**23, transcendentals=0),
    )(shifts, position, tile, tb, side, corner)


def exchange_kernel(count_y, count_x, send_ref, code_ref, got_ref, got_code_ref, sems, code_sems, own_sems):
    devices = count_y * count_x
    capacity = send_ref.shape[0] // devices
    me = lax.axis_index("ty") * count_x + lax.axis_index("tx")
    barrier = pltpu.get_barrier_semaphore()

    def at(peer):
        return (peer // count_x, peer % count_x)

    def greet(d, carry):
        pl.semaphore_signal(
            barrier, inc=1, device_id=at((me + d) % devices), device_id_type=pl.DeviceIdType.MESH
        )
        return carry

    lax.fori_loop(1, devices, greet, 0)
    pl.semaphore_wait(barrier, devices - 1)

    def copies(source, target, peer):
        block = pl.ds(source * capacity, capacity)
        landing = pl.ds(target * capacity, capacity)
        pieces = pltpu.make_async_remote_copy(
            src_ref=send_ref.at[block],
            dst_ref=got_ref.at[landing],
            send_sem=sems.at[0, source],
            recv_sem=sems.at[1, target],
            device_id=at(peer),
            device_id_type=pl.DeviceIdType.MESH,
        )
        codes = pltpu.make_async_remote_copy(
            src_ref=code_ref.at[source],
            dst_ref=got_code_ref.at[target],
            send_sem=code_sems.at[0, source],
            recv_sem=code_sems.at[1, target],
            device_id=at(peer),
            device_id_type=pl.DeviceIdType.MESH,
        )
        return pieces, codes

    def start(d, carry):
        peer = (me + d) % devices
        for copy in copies(peer, me, peer):
            copy.start()
        return carry

    lax.fori_loop(1, devices, start, 0)
    mine = pl.ds(me * capacity, capacity)
    own = pltpu.make_async_copy(send_ref.at[mine], got_ref.at[mine], own_sems.at[0])
    own_code = pltpu.make_async_copy(code_ref.at[me], got_code_ref.at[me], own_sems.at[1])
    own.start()
    own_code.start()
    own.wait()
    own_code.wait()

    def finish(d, carry):
        peer = (me + d) % devices
        for copy in copies(peer, peer, peer):
            copy.wait_send()
            copy.wait_recv()
        return carry

    lax.fori_loop(1, devices, finish, 0)


def exchange(send, codes, count_y, count_x):
    devices = count_y * count_x
    vmem = pl.BlockSpec(memory_space=pltpu.VMEM)
    return pl.pallas_call(
        functools.partial(exchange_kernel, count_y, count_x),
        out_shape=[
            jax.ShapeDtypeStruct(send.shape, send.dtype),
            jax.ShapeDtypeStruct(codes.shape, codes.dtype),
        ],
        in_specs=[vmem, vmem],
        out_specs=[pl.BlockSpec(memory_space=pl.ANY), vmem],
        scratch_shapes=[
            pltpu.SemaphoreType.DMA((2, devices)),
            pltpu.SemaphoreType.DMA((2, devices)),
            pltpu.SemaphoreType.DMA((2,)),
        ],
        name="exchange",
        compiler_params=pltpu.CompilerParams(
            collective_id=0, has_side_effects=True, vmem_limit_bytes=12 * 2**20
        ),
        cost_estimate=pl.CostEstimate(flops=0, bytes_accessed=2**23, transcendentals=0),
    )(send, codes)


def join_kernel(slot_ref, code_ref, patch_ref, got_ref, joined_ref, quads_ref, acc_ref, sum_ref, mean_ref, denom_ref):
    acc_ref[...] = jnp.zeros_like(acc_ref)
    step = 8

    def add(i, carry):
        for j in range(step):
            slot = slot_ref[i * step + j]
            acc_ref[slot] = acc_ref[slot] + got_ref[i * step + j].astype(F32)
        return carry

    lax.fori_loop(0, got_ref.shape[0] // step, add, 0)
    codes = code_ref[...]
    number = codes.shape[1]
    grid = patch_ref.shape[1]
    slot_marks = (codes % CODE == iota((SLOTS, number), 0)).astype(BF16)
    place_marks = (codes // CODE == iota((grid, number), 0)).astype(BF16)
    counts = mm_t(slot_marks, place_marks).astype(BF16)
    for y in range(SIDE):
        denom_ref[pl.ds(y, SLOTS, stride=SIDE), :] = mm(counts, patch_ref[y])
    row = iota((LANES, LANES), 0)
    column = iota((LANES, LANES), 1)
    half = SIDE // 2
    pool_one = ((row // (2 * SIDE)) * half + (row % SIDE) // 2 == column).astype(BF16)
    pool_two = (((row % half) // 2 == column) & (row < SIDE)).astype(BF16)
    batch = SLOTS // 4
    rows = batch * SIDE
    for c in range(SLOTS // batch):
        part = pl.ds(c * batch, batch)
        denom = jnp.maximum(denom_ref[pl.ds(c * rows, rows), :], 1.0)
        value = (acc_ref[part].reshape(rows, LANES) / denom).astype(BF16)
        mean_ref[...] = value.astype(F32)
        sum_ref[...] = mm(value, pool_one)
        level = (sum_ref[pl.ds(0, rows // 2, stride=2), :] + sum_ref[pl.ds(1, rows // 2, stride=2), :]) * 0.125
        sum_ref[pl.ds(0, rows // 2), :] = mm(level.astype(BF16), pool_two)
        quads_ref[pl.ds(c * rows // 4, rows // 4), :] = (
            sum_ref[pl.ds(0, rows // 4, stride=2), :] + sum_ref[pl.ds(1, rows // 4, stride=2), :]
        ) * 0.125
        parts = [mean_ref[pl.ds(j, rows // GROUPS, stride=GROUPS), :] for j in range(GROUPS)]
        high = SIDE // GROUPS
        for g, piece in enumerate(swap_groups(parts)):
            joined_ref[part, pl.ds(g * high, high), :] = piece.reshape(batch, high, LANES).astype(BF16)


def join(slots, codes, patches, got):
    vmem = pl.BlockSpec(memory_space=pltpu.VMEM)
    smem = pl.BlockSpec(memory_space=pltpu.SMEM)
    return pl.pallas_call(
        join_kernel,
        out_shape=[
            jax.ShapeDtypeStruct((SLOTS, SIDE, LANES), BF16),
            jax.ShapeDtypeStruct((SLOTS * SIDE // 4, LANES), F32),
        ],
        in_specs=[smem, vmem, vmem, vmem],
        out_specs=[vmem, vmem],
        scratch_shapes=[
            pltpu.VMEM((SLOTS + 1, SIDE, LANES), F32),
            pltpu.VMEM((SLOTS // 4 * SIDE, LANES), F32),
            pltpu.VMEM((SLOTS // 4 * SIDE, LANES), F32),
            pltpu.VMEM((SLOTS * SIDE, LANES), F32),
        ],
        name="join",
        compiler_params=pltpu.CompilerParams(vmem_limit_bytes=16 * 2**20),
        cost_estimate=pl.CostEstimate(flops=10**8, bytes_accessed=2**23, transcendentals=0),
    )(slots, codes, patches, got)


def assemble(quadrant_blocks):
    count, height, width = quadrant_blocks.shape
    shaped = quadrant_blocks.reshape(count // 4, 2, 2, height, width).transpose(0, 1, 3, 2, 4)
    return shaped.reshape(count // 4, 4 * height * width)


def patch_weights(length, depth, after):
    grid_side = length // SIDE
    ramps = ramp((1, length), 1, length).reshape(grid_side, SIDE)
    ramps, _ = lax.optimization_barrier((ramps, after))
    down = jnp.repeat(ramps, grid_side, axis=0).T
    across = jnp.tile(ramps, (grid_side, depth))
    return (down[:, :, None] * across[None]).astype(BF16)


def per_device(tiles, shifts, piece_target, coarse_target):
    tile = tiles[0, 0]
    count_y = lax.axis_size("ty")
    count_x = lax.axis_size("tx")
    devices = count_y * count_x
    depth, length, _ = tile.shape
    pieces_n = (length // SIDE) ** 2
    capacity = 2 * pieces_n // devices

    targets = piece_target[0, 0]
    owners = targets // SLOTS
    order = jnp.arange(pieces_n, dtype=jnp.int32)
    earlier = (owners[:, None] == owners[None, :]) & (order[None, :] < order[:, None])
    position = owners * capacity + jnp.sum(earlier.astype(jnp.int32), axis=1)
    codes = order * CODE + targets % SLOTS - SLOTS
    rows = jnp.arange(devices * capacity, dtype=jnp.int32)
    send_codes = SLOTS + jnp.sum(
        jnp.where(position[None, :] == rows[:, None], codes[None, :], 0), axis=1
    )
    send_codes = jnp.broadcast_to(send_codes.reshape(devices, 1, capacity), (devices, 8, capacity))
    send_codes = jnp.pad(send_codes, ((0, 0), (0, 0), (0, LANES - capacity)))

    top = shifted(tile[:, length - H :, :], "ty", 1)
    bottom = shifted(tile[:, :H, :], "ty", -1)
    tb = jnp.concatenate([top, bottom], axis=1)
    last = jnp.concatenate([tile[:, :, length - H :], tb[:, :, length - H :]], axis=1)
    first = jnp.concatenate([tile[:, :, :H], tb[:, :, :H]], axis=1)
    last, first = last.transpose(0, 2, 1), first.transpose(0, 2, 1)
    left = shifted(last, "tx", 1)
    right = shifted(first, "tx", -1)
    side = jnp.concatenate([left, right], axis=1)
    right_bins, left_bins, bottom_bins, top_bins = all_bins(tile, first)
    next_left = shifted(left_bins, "tx", -1)
    next_top = shifted(top_bins, "ty", -1)
    send = make_pieces(
        shifts[0, 0], position, tile, tb, side[:, :, :length], side[:, :, length:], devices * capacity
    )
    corr_right, corr_below = phase_surfaces(right_bins, next_left, bottom_bins, next_top)
    patches = patch_weights(length, depth, tb)
    got, got_codes = exchange(send, send_codes, count_y, count_x)
    codes = got_codes[:, 0, :capacity].reshape(-1)

    coarse_ids = coarse_target[0, 0]
    owner = coarse_ids // SLOTS
    per_peer = SLOTS // count_x
    number = jnp.arange(SLOTS, dtype=jnp.int32)
    ahead = (owner[:, None] == owner[None, :]) & (number[None, :] < number[:, None])
    coarse_pos = owner * per_peer + jnp.sum(ahead.astype(jnp.int32), axis=1)
    ordering = (coarse_pos[None, :] == number[:, None]).astype(BF16)
    locals_ = jnp.broadcast_to((coarse_ids % SLOTS).astype(BF16)[:, None], (SLOTS, SLOTS))
    joined, quads = join(codes % CODE, codes[None, :], patches, got)
    joined = joined.reshape(SLOTS, depth * SIDE * SIDE)
    flat = quads[:, : SIDE // 4].astype(BF16).reshape(SLOTS, -1)
    send_quads = mm(ordering, jnp.concatenate([flat, locals_], axis=1)).astype(BF16)
    got_quads = lax.all_to_all(send_quads, "tx", split_axis=0, concat_axis=0, tiled=True)
    width = flat.shape[1]
    got_local = got_quads[:, width].astype(jnp.int32)
    place = (got_local[None, :] == number[:, None]).astype(BF16)
    placed = mm(place, got_quads[:, :width]).reshape(SLOTS, SIDE // 4, SIDE // 4)
    coarse = assemble(placed).astype(BF16)
    return (joined, coarse, corr_right, corr_below)


def solution(mesh):
    placed = (
        P("ty", "tx", None, None, None),
        P("ty", "tx", None),
        P("ty", "tx", None),
        P("ty", "tx", None),
    )
    return jax.shard_map(
        per_device,
        mesh=mesh,
        in_specs=placed,
        out_specs=(P(("ty", "tx"), None), P(("ty", "tx"), None), P("ty", "tx"), P("ty", "tx")),
        check_vma=False,
    )
```

```python
import functools
import math

import jax
import jax.numpy as jnp
from jax import lax
from jax.experimental import pallas as pl
from jax.experimental.pallas import tpu as pltpu
from jax.sharding import PartitionSpec as P

SIDE = 32
OV = 48
H = 8
SLOTS = 64
CODE = 2 * SLOTS
LANES = 128
GROUPS = LANES // SIDE
F32 = jnp.float32
BF16 = jnp.bfloat16


def shifted(value, axis, steps):
    count = lax.axis_size(axis)
    first, last = (max(0, -steps), min(count, count - steps))
    return lax.ppermute(value, axis, [(source, source + steps) for source in range(first, last)])


def highest(left, right):
    return jnp.dot(left, right, precision=lax.Precision.HIGHEST, preferred_element_type=F32)


def iota(shape, dim):
    return lax.broadcasted_iota(jnp.int32, shape, dim)


def mm(a, b):
    return jnp.dot(a, b, preferred_element_type=F32)


def mm_t(a, b):
    return lax.dot_general(a, b, (((1,), (1,)), ((), ())), preferred_element_type=F32)


def bins_kernel(tile_ref, right_ref, left_ref, bottom_ref, top_ref):
    depth, length, _ = tile_ref.shape
    bins = OV // 4
    scale = 1.0 / math.sqrt(16.0 * depth)
    pool = (iota((length, length // 4), 0) // 4 == iota((length, length // 4), 1)).astype(F32)
    first = (iota((16, LANES), 1) // 4 == iota((16, LANES), 0)).astype(BF16)
    last = ((iota((16, LANES), 1) - (LANES - OV)) // 4 == iota((16, LANES), 0)) & (
        iota((16, LANES), 1) >= LANES - OV
    )
    last = last.astype(BF16)
    left = right = top = bottom = jnp.zeros((16, length), F32)
    for z in range(depth):
        left += mm_t(first, tile_ref[z, :, :LANES])
        right += mm_t(last, tile_ref[z, :, length - LANES :])
        top += mm(first, tile_ref[z, :LANES, :])
        bottom += mm(last, tile_ref[z, length - LANES :, :])
    for ref, value in ((right_ref, right), (left_ref, left), (bottom_ref, bottom), (top_ref, top)):
        ref[...] = highest(value, pool)[:bins] * scale


def all_bins(tile):
    length = tile.shape[1]
    shape = jax.ShapeDtypeStruct((OV // 4, length // 4), F32)
    vmem = pl.BlockSpec(memory_space=pltpu.VMEM)
    return pl.pallas_call(
        bins_kernel,
        out_shape=[shape] * 4,
        in_specs=[vmem],
        out_specs=[vmem] * 4,
        name="bins",
        cost_estimate=pl.CostEstimate(flops=10**8, bytes_accessed=2**21, transcendentals=0),
    )(tile)


def dft_tables(length):
    index = jnp.arange(length, dtype=jnp.int32)
    product = index[:, None] * index[None, :] % length
    angle = product.astype(F32) * (2.0 * math.pi / length)
    norm = 1.0 / math.sqrt(length)
    return (jnp.cos(angle) * norm, jnp.sin(angle) * norm)


def phase_kernel(ca_ref, sa_ref, cb_ref, sb_ref, r_ref, l_ref, b_ref, t_ref, right_ref, below_ref):
    cos_a, sin_a, cos_b, sin_b = ca_ref[...], sa_ref[...], cb_ref[...], sb_ref[...]

    def spectrum(values):
        left_cos = highest(cos_a, values)
        left_sin = highest(sin_a, values)
        re = highest(left_cos, cos_b) - highest(left_sin, sin_b)
        im = -(highest(left_cos, sin_b) + highest(left_sin, cos_b))
        return (re, im)

    for own_ref, other_ref, out_ref in ((r_ref, l_ref, right_ref), (b_ref, t_ref, below_ref)):
        own_re, own_im = spectrum(own_ref[...])
        other_re, other_im = spectrum(other_ref[...])
        cross_re = own_re * other_re + own_im * other_im
        cross_im = own_im * other_re - own_re * other_im
        scale = 1.0 / jnp.sqrt(cross_re * cross_re + cross_im * cross_im + 1.0)
        normed_re = cross_re * scale
        normed_im = cross_im * scale
        out = highest(highest(cos_a, normed_re) - highest(sin_a, normed_im), cos_b)
        out = out - highest(highest(sin_a, normed_re) + highest(cos_a, normed_im), sin_b)
        out_ref[...] = out


def phase_surfaces(right, left, bottom, top):
    rows, columns = right.shape
    pad = 16 - rows
    cos_a, sin_a = (jnp.pad(t, ((0, pad), (0, pad))) for t in dft_tables(rows))
    cos_b, sin_b = dft_tables(columns)
    padded = [jnp.pad(v, ((0, pad), (0, 0))) for v in (right, left, bottom, top)]
    vmem = pl.BlockSpec(memory_space=pltpu.VMEM)
    out = pl.pallas_call(
        phase_kernel,
        out_shape=[jax.ShapeDtypeStruct((16, columns), F32)] * 2,
        in_specs=[vmem] * 8,
        out_specs=[vmem] * 2,
        name="phase",
        cost_estimate=pl.CostEstimate(flops=10**8, bytes_accessed=2**18, transcendentals=4096),
    )(cos_a, sin_a, cos_b, sin_b, *padded)
    return out[0][:rows], out[1][:rows]


def swap_groups(parts):
    group = iota(parts[0].shape, 1) // SIDE

    def pick(choices):
        value = choices[3]
        for g in range(3):
            value = jnp.where(group == g, choices[g], value)
        return value

    turned = []
    for d in range(GROUPS):
        mixed = pick([parts[(g + d) % GROUPS] for g in range(GROUPS)])
        turned.append(pltpu.roll(mixed, d * SIDE, 1) if d else mixed)
    return [pick([turned[(j - g) % GROUPS] for j in range(GROUPS)]) for g in range(GROUPS)]


def taps(offset, shape, out_dim, column):
    whole, frac = offset
    at = iota(shape, out_dim) + whole + H
    return (
        jnp.where(column == at, 1.0 - frac, 0.0) + jnp.where(column == at + 1, frac, 0.0)
    ).astype(BF16)


def split_shift(shift):
    whole = lax.shift_right_arithmetic(shift, 2)
    return whole, (shift - 4 * whole).astype(F32) * 0.25


def ramp(shape, dim, length):
    index = iota(shape, dim)
    nearest = jnp.minimum(jnp.minimum(index + 1, length - index), OV).astype(F32)
    return 1.0 + 3.0 * nearest / OV


def pieces_kernel(shift_ref, pos_ref, tile_ref, tb_ref, side_ref, corner_ref, send_ref, work_ref):
    depth, length, _ = tile_ref.shape

    def edge_column(shape, dim):
        c = iota(shape, dim)
        return jnp.where(c < H, c, c + length)

    sy, sx = split_shift(shift_ref[0]), split_shift(shift_ref[1])
    full, thin, wide = (length, length), (length, 2 * H), (2 * H, length)
    ry = taps(sy, full, 0, iota(full, 1) + H)
    ry_edge = taps(sy, thin, 0, edge_column(thin, 1))
    rx = taps(sx, full, 1, iota(full, 0) + H)
    rx_edge = taps(sx, wide, 1, edge_column(wide, 0))
    weights = ramp((length, 1), 0, length) * ramp((1, length), 1, length)
    for z in range(depth):
        along = (mm(ry, tile_ref[z]) + mm(ry_edge, tb_ref[z])).astype(BF16)
        along_side = (mm_t(ry, side_ref[z]) + mm_t(ry_edge, corner_ref[z])).astype(BF16)
        resampled = mm(along, rx) + mm(along_side, rx_edge)
        work_ref[z] = weights * resampled
    send_ref[...] = jnp.zeros_like(send_ref)
    grid_side = length // SIDE

    def row(py, carry):
        start = pl.multiple_of(py * SIDE, SIDE)
        for q in range(length // LANES):
            parts = [work_ref[z, pl.ds(start, SIDE), q * LANES : (q + 1) * LANES] for z in range(depth)]
            for g, piece in enumerate(swap_groups(parts)):
                send_ref[pos_ref[py * grid_side + q * GROUPS + g]] = piece.astype(BF16)
        return carry

    lax.fori_loop(0, grid_side, row, 0)


def make_pieces(shifts, position, tile, tb, side, corner, rows):
    vmem = pl.BlockSpec(memory_space=pltpu.VMEM)
    smem = pl.BlockSpec(memory_space=pltpu.SMEM)
    return pl.pallas_call(
        pieces_kernel,
        out_shape=jax.ShapeDtypeStruct((rows, SIDE, LANES), BF16),
        in_specs=[smem, smem, vmem, vmem, vmem, vmem],
        out_specs=vmem,
        scratch_shapes=[pltpu.VMEM(tile.shape, F32)],
        name="pieces",
        compiler_params=pltpu.CompilerParams(vmem_limit_bytes=40 * 2**20),
        cost_estimate=pl.CostEstimate(flops=2 * 10**9, bytes_accessed=2**23, transcendentals=0),
    )(shifts, position, tile, tb, side, corner)


def exchange_kernel(count_y, count_x, send_ref, code_ref, got_ref, got_code_ref, sems, code_sems, own_sems):
    devices = count_y * count_x
    capacity = send_ref.shape[0] // devices
    me = lax.axis_index("ty") * count_x + lax.axis_index("tx")
    barrier = pltpu.get_barrier_semaphore()

    def at(peer):
        return (peer // count_x, peer % count_x)

    def greet(d, carry):
        pl.semaphore_signal(
            barrier, inc=1, device_id=at((me + d) % devices), device_id_type=pl.DeviceIdType.MESH
        )
        return carry

    lax.fori_loop(1, devices, greet, 0)
    pl.semaphore_wait(barrier, devices - 1)

    def copies(source, target, peer):
        block = pl.ds(source * capacity, capacity)
        landing = pl.ds(target * capacity, capacity)
        pieces = pltpu.make_async_remote_copy(
            src_ref=send_ref.at[block],
            dst_ref=got_ref.at[landing],
            send_sem=sems.at[0, source],
            recv_sem=sems.at[1, target],
            device_id=at(peer),
            device_id_type=pl.DeviceIdType.MESH,
        )
        codes = pltpu.make_async_remote_copy(
            src_ref=code_ref.at[source],
            dst_ref=got_code_ref.at[target],
            send_sem=code_sems.at[0, source],
            recv_sem=code_sems.at[1, target],
            device_id=at(peer),
            device_id_type=pl.DeviceIdType.MESH,
        )
        return pieces, codes

    def start(d, carry):
        peer = (me + 11 * d) % devices
        for copy in copies(peer, me, peer):
            copy.start()
        return carry

    lax.fori_loop(1, devices, start, 0)
    mine = pl.ds(me * capacity, capacity)
    own = pltpu.make_async_copy(send_ref.at[mine], got_ref.at[mine], own_sems.at[0])
    own_code = pltpu.make_async_copy(code_ref.at[me], got_code_ref.at[me], own_sems.at[1])
    own.start()
    own_code.start()
    own.wait()
    own_code.wait()

    def finish(d, carry):
        peer = (me + d) % devices
        for copy in copies(peer, peer, peer):
            copy.wait_send()
            copy.wait_recv()
        return carry

    lax.fori_loop(1, devices, finish, 0)


def exchange(send, codes, count_y, count_x):
    devices = count_y * count_x
    vmem = pl.BlockSpec(memory_space=pltpu.VMEM)
    return pl.pallas_call(
        functools.partial(exchange_kernel, count_y, count_x),
        out_shape=[
            jax.ShapeDtypeStruct(send.shape, send.dtype),
            jax.ShapeDtypeStruct(codes.shape, codes.dtype),
        ],
        in_specs=[vmem, vmem],
        out_specs=[vmem, vmem],
        scratch_shapes=[
            pltpu.SemaphoreType.DMA((2, devices)),
            pltpu.SemaphoreType.DMA((2, devices)),
            pltpu.SemaphoreType.DMA((2,)),
        ],
        name="exchange",
        compiler_params=pltpu.CompilerParams(
            collective_id=0, has_side_effects=True, vmem_limit_bytes=24 * 2**20
        ),
        cost_estimate=pl.CostEstimate(flops=0, bytes_accessed=2**23, transcendentals=0),
    )(send, codes)


def join_kernel(slot_ref, code_ref, patch_ref, got_ref, joined_ref, quads_ref, acc_ref, sum_ref, mean_ref, denom_ref):
    acc_ref[...] = jnp.zeros_like(acc_ref)
    step = 8

    def add(i, carry):
        for j in range(step):
            slot = slot_ref[i * step + j]
            acc_ref[slot] = acc_ref[slot] + got_ref[i * step + j].astype(F32)
        return carry

    lax.fori_loop(0, got_ref.shape[0] // step, add, 0)
    codes = code_ref[...]
    number = codes.shape[1]
    grid = patch_ref.shape[1]
    slot_marks = (codes % CODE == iota((SLOTS, number), 0)).astype(BF16)
    place_marks = (codes // CODE == iota((grid, number), 0)).astype(BF16)
    counts = mm_t(slot_marks, place_marks).astype(BF16)
    for y in range(SIDE):
        denom_ref[pl.ds(y, SLOTS, stride=SIDE), :] = mm(counts, patch_ref[y])
    row = iota((LANES, LANES), 0)
    column = iota((LANES, LANES), 1)
    half = SIDE // 2
    pool_one = ((row // (2 * SIDE)) * half + (row % SIDE) // 2 == column).astype(BF16)
    pool_two = (((row % half) // 2 == column) & (row < SIDE)).astype(BF16)
    batch = SLOTS // 4
    rows = batch * SIDE
    for c in range(SLOTS // batch):
        part = pl.ds(c * batch, batch)
        denom = jnp.maximum(denom_ref[pl.ds(c * rows, rows), :], 1.0)
        value = (acc_ref[part].reshape(rows, LANES) / denom).astype(BF16)
        mean_ref[...] = value.astype(F32)
        sum_ref[...] = mm(value, pool_one)
        level = (sum_ref[pl.ds(0, rows // 2, stride=2), :] + sum_ref[pl.ds(1, rows // 2, stride=2), :]) * 0.125
        sum_ref[pl.ds(0, rows // 2), :] = mm(level.astype(BF16), pool_two)
        quads_ref[pl.ds(c * rows // 4, rows // 4), :] = (
            sum_ref[pl.ds(0, rows // 4, stride=2), :] + sum_ref[pl.ds(1, rows // 4, stride=2), :]
        ) * 0.125
        parts = [mean_ref[pl.ds(j, rows // GROUPS, stride=GROUPS), :] for j in range(GROUPS)]
        high = SIDE // GROUPS
        for g, piece in enumerate(swap_groups(parts)):
            joined_ref[part, pl.ds(g * high, high), :] = piece.reshape(batch, high, LANES).astype(BF16)


def join(slots, codes, patches, got):
    vmem = pl.BlockSpec(memory_space=pltpu.VMEM)
    smem = pl.BlockSpec(memory_space=pltpu.SMEM)
    return pl.pallas_call(
        join_kernel,
        out_shape=[
            jax.ShapeDtypeStruct((SLOTS, SIDE, LANES), BF16),
            jax.ShapeDtypeStruct((SLOTS * SIDE // 4, LANES), F32),
        ],
        in_specs=[smem, vmem, vmem, vmem],
        out_specs=[vmem, vmem],
        scratch_shapes=[
            pltpu.VMEM((SLOTS + 1, SIDE, LANES), F32),
            pltpu.VMEM((SLOTS // 4 * SIDE, LANES), F32),
            pltpu.VMEM((SLOTS // 4 * SIDE, LANES), F32),
            pltpu.VMEM((SLOTS * SIDE, LANES), F32),
        ],
        name="join",
        compiler_params=pltpu.CompilerParams(vmem_limit_bytes=32 * 2**20),
        cost_estimate=pl.CostEstimate(flops=10**8, bytes_accessed=2**23, transcendentals=0),
    )(slots, codes, patches, got)


def assemble(quadrant_blocks):
    count, height, width = quadrant_blocks.shape
    shaped = quadrant_blocks.reshape(count // 4, 2, 2, height, width).transpose(0, 1, 3, 2, 4)
    return shaped.reshape(count // 4, 4 * height * width)


def patch_weights(length, depth):
    grid_side = length // SIDE
    ramps = ramp((1, length), 1, length).reshape(grid_side, SIDE)
    down = jnp.repeat(ramps, grid_side, axis=0).T
    across = jnp.tile(ramps, (grid_side, depth))
    return (down[:, :, None] * across[None]).astype(BF16)


def per_device(tiles, shifts, piece_target, coarse_target):
    tile = tiles[0, 0]
    count_y = lax.axis_size("ty")
    count_x = lax.axis_size("tx")
    devices = count_y * count_x
    depth, length, _ = tile.shape
    pieces_n = (length // SIDE) ** 2
    capacity = 2 * pieces_n // devices

    targets = piece_target[0, 0]
    owners = targets // SLOTS
    order = jnp.arange(pieces_n, dtype=jnp.int32)
    earlier = (owners[:, None] == owners[None, :]) & (order[None, :] < order[:, None])
    position = owners * capacity + jnp.sum(earlier.astype(jnp.int32), axis=1)
    codes = order * CODE + targets % SLOTS - SLOTS
    rows = jnp.arange(devices * capacity, dtype=jnp.int32)
    send_codes = SLOTS + jnp.sum(
        jnp.where(position[None, :] == rows[:, None], codes[None, :], 0), axis=1
    )
    send_codes = jnp.broadcast_to(send_codes.reshape(devices, 1, capacity), (devices, 8, capacity))
    send_codes = jnp.pad(send_codes, ((0, 0), (0, 0), (0, LANES - capacity)))

    top = shifted(tile[:, length - H :, :], "ty", 1)
    bottom = shifted(tile[:, :H, :], "ty", -1)
    tb = jnp.concatenate([top, bottom], axis=1)
    last = jnp.concatenate([tile[:, :, length - H :], tb[:, :, length - H :]], axis=1)
    first = jnp.concatenate([tile[:, :, :H], tb[:, :, :H]], axis=1)
    left = shifted(last.transpose(0, 2, 1), "tx", 1)
    right = shifted(first.transpose(0, 2, 1), "tx", -1)
    side = jnp.concatenate([left, right], axis=1)
    right_bins, left_bins, bottom_bins, top_bins = all_bins(tile)
    next_left = shifted(left_bins, "tx", -1)
    next_top = shifted(top_bins, "ty", -1)
    send = make_pieces(
        shifts[0, 0], position, tile, tb, side[:, :, :length], side[:, :, length:], devices * capacity
    )
    corr_right, corr_below = phase_surfaces(right_bins, next_left, bottom_bins, next_top)
    patches = patch_weights(length, depth)
    got, got_codes = exchange(send, send_codes, count_y, count_x)
    codes = got_codes[:, 0, :capacity].reshape(-1)

    coarse_ids = coarse_target[0, 0]
    owner = coarse_ids // SLOTS
    per_peer = SLOTS // count_x
    number = jnp.arange(SLOTS, dtype=jnp.int32)
    ahead = (owner[:, None] == owner[None, :]) & (number[None, :] < number[:, None])
    coarse_pos = owner * per_peer + jnp.sum(ahead.astype(jnp.int32), axis=1)
    ordering = (coarse_pos[None, :] == number[:, None]).astype(BF16)
    locals_ = jnp.broadcast_to((coarse_ids % SLOTS).astype(BF16)[:, None], (SLOTS, SLOTS))
    joined, quads = join(codes % CODE, codes[None, :], patches, got)
    joined = joined.reshape(SLOTS, depth * SIDE * SIDE)
    flat = quads[:, : SIDE // 4].astype(BF16).reshape(SLOTS, -1)
    send_quads = mm(ordering, jnp.concatenate([flat, locals_], axis=1)).astype(BF16)
    got_quads = lax.all_to_all(send_quads, "tx", split_axis=0, concat_axis=0, tiled=True)
    width = flat.shape[1]
    got_local = got_quads[:, width].astype(jnp.int32)
    place = (got_local[None, :] == number[:, None]).astype(BF16)
    placed = mm(place, got_quads[:, :width]).reshape(SLOTS, SIDE // 4, SIDE // 4)
    coarse = assemble(placed).astype(BF16)
    return (joined, coarse, corr_right, corr_below)


def solution(mesh):
    placed = (
        P("ty", "tx", None, None, None),
        P("ty", "tx", None),
        P("ty", "tx", None),
        P("ty", "tx", None),
    )
    return jax.shard_map(
        per_device,
        mesh=mesh,
        in_specs=placed,
        out_specs=(P(("ty", "tx"), None), P(("ty", "tx"), None), P("ty", "tx"), P("ty", "tx")),
        check_vma=False,
    )
```
